256 devices in a mesh: seq: 32 (over x, z), exp: 8 (over y, core).
Axes of the slice: x: 4, y: 4, z: 8, core: 2. Of those that a mesh axis runs over, the one named last changes fastest.
Arguments:
- queries: bfloat16 [4, 64, 1536], P(None, 'exp'), may hold values from -200 to 200
- new_key_value: bfloat16 [4, 64, 2, 512], P(None, 'exp'), may hold values from -8 to 8
- key_value_cache: bfloat16 [64, 256, 64, 2, 512], P('exp', 'seq'), may hold values from -8 to 8
- page_table: int32 [64, 256], P('exp', 'seq'), may hold values from 0 to 63, as said below
- cache_len: int32 [64], P('exp'), may hold values from 1 to 16384
- routes: int32 [4, 64, 8], P(None, 'exp'), may hold values from 0 to 39, all different within a row; in each aligned block of 8 rows (0 to 7, 8 to 15, ..., all dimensions but the last counted through in order) at most 4 rows name the same one
- residual: bfloat16 [4, 64, 1536], P(None, 'exp', 'seq'), may hold values from -8 to 8
- w_out: bfloat16 [1536, 1536], P(None, 'seq'), may hold values from -0.15625 to 0.15625
- norm_gain: float32 [1536], P('seq'), may hold values from 0.1 to 1.9
- w_router: bfloat16 [1536, 40], P('seq'), may hold values from -0.15625 to 0.15625
- w_gate_up: bfloat16 [40, 1536, 2, 512], P('exp', 'seq'), may hold values from -0.15625 to 0.15625
- w_down: bfloat16 [40, 1536, 512], P('exp', 'seq'), may hold values from -0.25 to 0.25
Outputs:
- layer_out: bfloat16 [4, 64, 1536], P(None, 'exp', 'seq')
The draws below stay inside these ranges and needn't reach their ends.
Inputs may be any that keep to these rules, and one draw needn't show every extreme that they name: `page_table`: within the block of one index of exp and one index of seq (8 rows, 8 columns) the entries are each page slot once. `routes`: in each step the 8 tokens of one index of exp name one expert at most 4 times; a row's 8 experts differ.
All inputs are finite; a program needn't handle non-finite values.
Results may differ from the reference program's by a relative error of at most 0.0053.
Values may be sent and summed in bfloat16 or wider, within the bound.
A program may use at most 128 MiB of HBM per device.

```python
import math
import jax
import jax.numpy as jnp
import numpy as np
from jax import lax

D = 1536
QUERY_HEADS = 24
KEY_VALUE_HEADS = 8
HEAD_SIZE = 64
EXPERTS = 40
FF = 512
TOPK = 8
REQ_DEV = 8
SHARD_POSITIONS = 512
PAGE_POSITIONS = 64
DECODE_STEPS = 4
REQUEST_COUNT = 64
PAGES_PER_SHARD = 8
MAXLEN = 16384
CAP = 4
N_SEQ = 32


def drawn_keys(key):
    base_offset = jax.random.normal(jax.random.fold_in(key, 11), (DECODE_STEPS, REQUEST_COUNT, 2, KEY_VALUE_HEADS * HEAD_SIZE), jnp.float32) * 1.6
    base_offset = jnp.clip(base_offset, -8.0, 8.0)
    return base_offset


def draw_key_value_cache(key, part):
    page_count = MAXLEN // PAGE_POSITIONS
    shape = (REQUEST_COUNT, page_count, PAGE_POSITIONS, 2, KEY_VALUE_HEADS * HEAD_SIZE)
    base = jnp.clip(jax.random.normal(jax.random.fold_in(key, 61), shape, jnp.float32) * 1.6, -8.0, 8.0).astype(jnp.bfloat16)
    return base


def draw_new_key_value(key, part):
    base_offset = drawn_keys(jax.random.fold_in(key, 5))
    return base_offset.astype(jnp.bfloat16)


def draw_queries(key, part):
    noise_key = jax.random.fold_in(key, 21)
    drawn = jnp.clip(jax.random.normal(noise_key, (DECODE_STEPS, REQUEST_COUNT, QUERY_HEADS * HEAD_SIZE), jnp.float32) * 1.6, -8.0, 8.0)
    return drawn.astype(jnp.bfloat16)


def draw_page_table(key, part):
    exp_groups = REQUEST_COUNT // REQ_DEV
    seq_groups = MAXLEN // SHARD_POSITIONS
    block_keys = jax.random.split(key, exp_groups * seq_groups)
    orders = jax.vmap(lambda block_key: jax.random.permutation(block_key, REQ_DEV * PAGES_PER_SHARD))(block_keys)
    orders = orders.reshape(exp_groups, seq_groups, REQ_DEV, PAGES_PER_SHARD)
    orders = jnp.transpose(orders, (0, 2, 1, 3)).reshape(REQUEST_COUNT, seq_groups * PAGES_PER_SHARD)
    return orders.astype(jnp.int32)


def draw_cache_len(key, part):
    length_bits = MAXLEN.bit_length() - 1
    exponent = jax.random.randint(jax.random.fold_in(key, 41), (REQUEST_COUNT,), 4, length_bits + 1)
    ceiling = jnp.left_shift(jnp.ones((REQUEST_COUNT,), jnp.int32), exponent)
    lengths = jax.random.randint(jax.random.fold_in(key, 42), (REQUEST_COUNT,), 0, MAXLEN) % ceiling + 1
    longest = jax.random.randint(jax.random.fold_in(key, 43), (), 0, REQUEST_COUNT)
    lengths = jnp.where(jnp.arange(REQUEST_COUNT) == longest, MAXLEN, lengths)
    return lengths.astype(jnp.int32)


def draw_residual(key, part):
    column = jnp.arange(D, dtype=jnp.float32) / max(D - 1, 1)
    col_scale = 0.05 * 10.0 ** column * jnp.exp(jax.random.uniform(jax.random.fold_in(key, 31), (D,), jnp.float32, 0.0, math.log(2.0)))
    row_scale = jnp.exp(jax.random.uniform(jax.random.fold_in(key, 32), (DECODE_STEPS, REQUEST_COUNT, 1), jnp.float32, 0.0, math.log(3.0)))
    noise = jax.random.normal(jax.random.fold_in(key, 34), (DECODE_STEPS, REQUEST_COUNT, D), jnp.float32)
    return jnp.clip(noise * col_scale * row_scale, -8.0, 8.0).astype(jnp.bfloat16)


def level_of(own_key, shape, cuts, smallest, largest):
    loudness, own = 1.0, jax.random.fold_in(own_key, 6)
    for position, shards_of in cuts:
        steps = jnp.exp(jax.random.uniform(jax.random.fold_in(own, position), (shards_of,), jnp.float32, smallest / len(cuts), largest / len(cuts)))
        loudness = loudness * jnp.repeat(steps, shape[position] // shards_of).reshape([-1 if axis == position else 1 for axis in range(len(shape))])
    return loudness


def shared_out(key, own, number, rows, count, top, reach, lean):
    sequence = jax.random.permutation(key, count)
    crowded, common = shares(count, rows * top, reach, lean, True), shares(count, rows * top, reach, lean, False)
    places = jnp.arange(count)

    def named(sizes, turn):
        used = int((sizes > 0).sum())
        fixed = max(1, used // 4)
        moved = fixed + (places - fixed + turn * (used - fixed)) % max(1, count - fixed)
        return jnp.zeros((count,), jnp.int32).at[sequence[jnp.where(places < fixed, places, moved)]].set(jnp.asarray(sizes, jnp.int32))

    sizes = jnp.where(number % 4 == 0, named(crowded, number // 4), named(common, number - number // 4 - 1))
    mixed = jax.random.permutation(jax.random.fold_in(own, 3), count)
    donor, sink = mixed[0:count // 2 * 2:2], mixed[1:count // 2 * 2:2]
    room = jnp.minimum(sizes[donor] - 1, reach - sizes[sink]) // 2
    room = jnp.where((donor == sequence[0]) | (sink == sequence[0]) | (sizes[sink] == 0), 0, jnp.maximum(room, 0))
    moved = jax.random.randint(jax.random.fold_in(own, 4), (count // 2,), 0, 1 << 20) % (room + 1)
    sizes = sizes.at[donor].add(-moved).at[sink].add(moved)
    labels = jnp.searchsorted(jnp.cumsum(sizes), jnp.arange(rows * top), side="right").astype(jnp.int32)
    table = labels.reshape(top, rows).T
    table = table[jax.random.permutation(jax.random.fold_in(own, 1), rows)]
    turn = jax.random.randint(jax.random.fold_in(own, 2), (rows, 1), 0, top)
    return jnp.take_along_axis(table, (jnp.arange(top)[None, :] + turn) % top, axis=1)


def shares(number_of, total, bound, slope, full):
    weights = [(1 << 20) // math.isqrt(grade ** slope) + 1 for grade in range(1, number_of + 1)]
    largest = bound if full else min(bound, max(-(-total // number_of), total * weights[0] // sum(weights)))
    least = 1 if total - largest >= number_of - 1 else 0
    counts, spare = [largest] + [least] * (number_of - 1), total - largest - least * (number_of - 1)
    while spare > 0:
        free = [i for i in range(1, number_of) if counts[i] < largest] or [i for i in range(1, number_of) if counts[i] < bound]
        whole, budget = sum([weights[i] for i in free]), spare
        for i in free:
            more = min(bound - counts[i], max(1, budget * weights[i] // whole), spare)
            counts[i] = counts[i] + more
            spare = spare - more
    return np.array(counts)


def bell_draw(stream_key, shape, width, reach, shards=(), kind=jnp.bfloat16):
    drawn = width * jax.random.normal(stream_key, shape, jnp.float32)
    if shards:
        drawn = drawn * level_of(stream_key, shape, shards, -0.22, 0.18)
    return jnp.clip(drawn, -reach, reach).astype(kind)


def setup_inputs(seed: int = 0) -> dict:
    keys = jax.random.split(jax.random.key(seed), 13)
    queries = draw_queries(jax.random.fold_in(keys[12], 71), 0)
    new_key_value = draw_new_key_value(jax.random.fold_in(keys[12], 71), 0)
    key_value_cache = draw_key_value_cache(jax.random.fold_in(keys[12], 71), 0)
    page_table = draw_page_table(jax.random.fold_in(keys[12], 71), 0)
    cache_len = draw_cache_len(jax.random.fold_in(keys[12], 71), 0)
    routes_keys = jax.random.split(jax.random.fold_in(keys[5], 1), DECODE_STEPS * REQUEST_COUNT // REQ_DEV)
    routes_turns = jax.random.permutation(jax.random.fold_in(keys[5], 3), DECODE_STEPS * REQUEST_COUNT // REQ_DEV)
    routes = jax.vmap(lambda own, number: shared_out(jax.random.fold_in(keys[5], 2), own, number, REQ_DEV, EXPERTS, TOPK, CAP, 2))(routes_keys, routes_turns).reshape((DECODE_STEPS, REQUEST_COUNT, TOPK))
    residual = draw_residual(jax.random.fold_in(keys[12], 71), 0)
    w_out = bell_draw(keys[7], (QUERY_HEADS * HEAD_SIZE, D), (QUERY_HEADS * HEAD_SIZE) ** -0.5, 0.15625, ((1, 32),))
    norm_gain = jnp.clip(1.0 + 0.18 * jax.random.normal(keys[8], (D,), jnp.float32), 0.1, 1.9)
    w_router = bell_draw(keys[9], (D, EXPERTS), D ** -0.5, 0.15625, ((0, 32),))
    w_gate_up = bell_draw(keys[10], (EXPERTS, D, 2, FF), D ** -0.5, 0.15625, ((0, 8), (1, 32)))
    w_down = bell_draw(keys[11], (EXPERTS, D, FF), FF ** -0.5, 0.25, ((0, 8), (1, 32)))
    return dict(queries=queries, new_key_value=new_key_value, key_value_cache=key_value_cache, page_table=page_table, cache_len=cache_len, routes=routes, residual=residual, w_out=w_out, norm_gain=norm_gain, w_router=w_router, w_gate_up=w_gate_up, w_down=w_down)


NEG_FILL = -1e+30

def reference(queries, new_key_value, key_value_cache, page_table, cache_len, routes, residual, w_out, norm_gain, w_router, w_gate_up, w_down):
    query_head_group = QUERY_HEADS // KEY_VALUE_HEADS
    page_count = N_SEQ * PAGES_PER_SHARD
    step_ids = jnp.arange(DECODE_STEPS)
    causal = step_ids[None, :] <= step_ids[:, None]

    def attend(request_index):
        owner_group = request_index // REQ_DEV
        physical = page_table[request_index]
        row_ids = (owner_group * REQ_DEV + physical // PAGES_PER_SHARD).astype(jnp.int32)
        col_ids = (jnp.arange(page_count) // PAGES_PER_SHARD * PAGES_PER_SHARD + physical % PAGES_PER_SHARD).astype(jnp.int32)
        gathered_rows = key_value_cache[row_ids, col_ids]
        cached_key_rows = gathered_rows[:, :, 0].reshape(N_SEQ, SHARD_POSITIONS, KEY_VALUE_HEADS, HEAD_SIZE).astype(jnp.float32)
        cached_value_rows = gathered_rows[:, :, 1].reshape(N_SEQ, SHARD_POSITIONS, KEY_VALUE_HEADS, HEAD_SIZE).astype(jnp.float32)
        positions = jnp.arange(MAXLEN).reshape(N_SEQ, SHARD_POSITIONS)
        live_mask = (positions < cache_len[request_index])[None, None, None]
        current_query = queries[:, request_index].astype(jnp.float32).reshape(DECODE_STEPS, KEY_VALUE_HEADS, query_head_group, HEAD_SIZE)
        scores = jnp.einsum('tkgd,bskd->tkgbs', current_query, cached_key_rows) * 0.125
        scores = jnp.where(live_mask, scores, NEG_FILL)
        block_max = lax.optimization_barrier(jnp.max(scores, axis=-1))
        weights = jnp.where(live_mask, jnp.exp(scores - block_max[..., None]), 0.0)
        block_sum = lax.optimization_barrier(jnp.sum(weights, axis=-1))
        rounded = lax.optimization_barrier(weights.astype(jnp.bfloat16)).astype(jnp.float32)
        block_acc = jnp.einsum('tkgbs,bskd->tkgbd', rounded, cached_value_rows)
        new_key_rows = new_key_value[:, request_index, 0].astype(jnp.float32).reshape(DECODE_STEPS, KEY_VALUE_HEADS, HEAD_SIZE)
        new_value_rows = new_key_value[:, request_index, 1].astype(jnp.float32).reshape(DECODE_STEPS, KEY_VALUE_HEADS, HEAD_SIZE)
        fresh_scores = jnp.einsum('tkgd,ukd->tkgu', current_query, new_key_rows) * 0.125
        kept_mask = causal[:, None, None, :]
        fresh_scores = jnp.where(kept_mask, fresh_scores, NEG_FILL)
        fresh_max = lax.optimization_barrier(jnp.max(fresh_scores, axis=-1))
        fresh_weights = jnp.where(kept_mask, jnp.exp(fresh_scores - fresh_max[..., None]), 0.0)
        fresh_sum = lax.optimization_barrier(jnp.sum(fresh_weights, axis=-1))
        fresh_round = lax.optimization_barrier(fresh_weights.astype(jnp.bfloat16)).astype(jnp.float32)
        fresh_acc = jnp.einsum('tkgu,ukd->tkgd', fresh_round, new_value_rows)
        overall = jnp.maximum(lax.optimization_barrier(jnp.max(block_max, axis=-1)), fresh_max)
        block_scale = jnp.exp(block_max - overall[..., None])
        fresh_scale = jnp.exp(fresh_max - overall)
        numer = lax.optimization_barrier(jnp.sum(block_scale[..., None] * block_acc, axis=3)) + fresh_scale[..., None] * fresh_acc
        denom = lax.optimization_barrier(jnp.sum(block_scale * block_sum, axis=3)) + fresh_scale * fresh_sum
        return (numer / denom[..., None]).reshape(DECODE_STEPS, QUERY_HEADS * HEAD_SIZE)
    attention = lax.map(attend, jnp.arange(REQUEST_COUNT))
    attention = jnp.transpose(attention, (1, 0, 2)).astype(jnp.bfloat16).reshape(DECODE_STEPS * REQUEST_COUNT, QUERY_HEADS * HEAD_SIZE)
    hidden_state = residual.reshape(DECODE_STEPS * REQUEST_COUNT, D).astype(jnp.float32) + jnp.dot(attention, w_out, preferred_element_type=jnp.float32)
    inv_rms = lax.rsqrt(lax.optimization_barrier(jnp.mean(hidden_state * hidden_state, axis=-1)) + 1e-06)
    gain_f32 = norm_gain.astype(jnp.float32)
    scaled = (hidden_state * gain_f32).astype(jnp.bfloat16)
    logits = jnp.dot(scaled, w_router, preferred_element_type=jnp.float32) * inv_rms[:, None]
    normed = (hidden_state * gain_f32 * inv_rms[:, None]).astype(jnp.bfloat16)
    chosen_routes = routes.reshape(DECODE_STEPS * REQUEST_COUNT, TOPK)
    picked_logits = jnp.take_along_axis(logits, chosen_routes, axis=1)
    exp_logit = jnp.exp(picked_logits)
    gate_weights = exp_logit / lax.optimization_barrier(jnp.sum(exp_logit, axis=-1, keepdims=True))

    def one_expert(moe_total, expert):
        hit_mask = (chosen_routes == expert).astype(jnp.float32)
        weight = lax.optimization_barrier(jnp.sum(hit_mask * gate_weights, axis=-1))
        pre_act = jnp.dot(normed, w_gate_up[expert].reshape(D, 2 * FF), preferred_element_type=jnp.float32).reshape(-1, 2, FF)
        inner_act = (jax.nn.silu(pre_act[:, 0]) * pre_act[:, 1]).astype(jnp.bfloat16)
        outputs = jnp.dot(inner_act, w_down[expert].T, preferred_element_type=jnp.float32).astype(jnp.bfloat16)
        outputs = lax.optimization_barrier(outputs).astype(jnp.float32)
        return (moe_total + weight[:, None] * outputs, None)
    moe_total, unused_out = lax.scan(one_expert, jnp.zeros((DECODE_STEPS * REQUEST_COUNT, D), jnp.float32), jnp.arange(EXPERTS))
    return (hidden_state + moe_total).astype(jnp.bfloat16).reshape(DECODE_STEPS, REQUEST_COUNT, D)
```

```python
import jax
import jax.numpy as jnp
from jax import lax
from jax.experimental import pallas as pl
from jax.experimental.pallas import tpu as pltpu
from jax.sharding import PartitionSpec as P

NEG = -1e30
N_SEQ = 32
N_EXP = 8
STEPS = 4
REQS = 8
TOKENS = STEPS * REQS
EXPERTS = 40
EXPERTS_LOCAL = 5
UNITS = 20
SLICE = 48
D = 1536
ALL_TOKENS = TOKENS * N_EXP
F32 = jnp.float32
BF16 = jnp.bfloat16
MESH = pl.DeviceIdType.MESH
VMEM = pltpu.VMEM


def iota(shape, axis):
    return lax.broadcasted_iota(jnp.int32, shape, axis)


def nt_dot(a, b):
    return lax.dot_general(a, b, (((1,), (1,)), ((), ())), preferred_element_type=F32)


def nn_dot(a, b):
    return lax.dot_general(a, b, (((1,), (0,)), ((), ())), preferred_element_type=F32)


def spread_queries(q_ref, rows_ref):
    low = iota((REQS, 128), 1) < 64
    for t in range(STEPS):
        q = q_ref[t].astype(F32) * 0.125
        tiles = [q[:, 128 * i : 128 * i + 128] for i in range(12)]
        for g in range(3):
            for pair in range(4):
                first, second = 6 * pair + g, 6 * pair + 3 + g
                if g == 1:
                    tile = jnp.where(low, tiles[second // 2], tiles[first // 2])
                    tile = pltpu.roll(tile, 64, 1)
                else:
                    tile = jnp.where(low, tiles[first // 2], tiles[second // 2])
                base = g * 512 + pair * 128
                rows_ref[REQS * t : REQS * t + REQS, base : base + 128] = tile


def block_diagonal(rows_ref, row, g):
    own = iota((8, 512), 1) // 64 == iota((8, 512), 0)
    values = rows_ref[pl.ds(row, 1), 512 * g : 512 * g + 512]
    return jnp.where(own, jnp.broadcast_to(values, (8, 512)), 0.0)


def softmax_parts(queries, keys, values, live):
    scores = nt_dot(queries, keys)
    scores = jnp.where(live, scores, NEG)
    largest = jnp.max(scores, axis=1, keepdims=True)
    weights = jnp.where(live, jnp.exp(scores - largest), 0.0)
    total = jnp.sum(weights, axis=1, keepdims=True)
    acc = nn_dot(weights.astype(BF16), values)
    some = total > 0.0
    safe = jnp.where(some, total, 1.0)
    return acc / safe, jnp.where(some, largest + jnp.log(safe), NEG)


def message_tiles(out, lse, groups):
    out = out.reshape(groups, 8, 512)
    lse = lse.reshape(groups, 8, 1)
    head = iota((groups, 8, 128), 1)
    lane = iota((groups, 8, 128), 2)
    packed = out[:, :, 0:128]
    for j in range(1, 4):
        packed = jnp.where(head // 2 == j, out[:, :, 128 * j : 128 * j + 128], packed)
    packed = jnp.where(lane // 64 == head % 2, packed, 0.0)
    head, lane = head[0], lane[0]
    free = lane // 64 != head % 2
    place = lane % 64
    tiles = []
    for t in range(groups // 3):
        first = packed[3 * t] + pltpu.roll(packed[3 * t + 1], 64, 1)
        stat = jnp.where(place == 0, lse[3 * t], jnp.where(place == 1, lse[3 * t + 1], lse[3 * t + 2]))
        second = packed[3 * t + 2] + jnp.where(free & (place < 3), stat, 0.0)
        tiles.append((first, second))
    return tiles


def attend_kernel(table_ref, len_ref, q_ref, new_ref, kv_ref, out_ref, pages, rows, fresh, sems):
    seq = lax.axis_index("seq")

    def page_copy(r, j):
        return pltpu.make_async_copy(kv_ref.at[table_ref[r, j]], pages.at[r, j], sems.at[r, j])

    for r in range(REQS):
        for j in range(8):
            page_copy(r, j).start()
    spread_queries(q_ref, rows)

    t_own, r_own = lax.div(seq, 8), lax.rem(seq, 8)
    fresh[...] = jnp.zeros_like(fresh)
    for u in range(STEPS):
        for kind in range(2):
            fresh[kind, u : u + 1, :] = new_ref[u, r_own, kind : kind + 1, :].astype(F32)
    queries = jnp.concatenate([block_diagonal(rows, seq, g) for g in range(3)], axis=0).astype(BF16)
    live = iota((24, 16), 1) <= t_own
    out, lse = softmax_parts(queries, fresh[0].astype(BF16), fresh[1].astype(BF16), live)
    ((first, second),) = message_tiles(out, lse, 3)
    out_ref[N_SEQ, 0:8, :] = first
    out_ref[N_SEQ, 8:16, :] = second

    def body(r, carry):
        for j in range(8):
            page_copy(r, j).wait()
        keys = pages[r, :, :, 0, :].reshape(512, 512)
        values = pages[r, :, :, 1, :].reshape(512, 512)
        queries = jnp.concatenate(
            [block_diagonal(rows, REQS * t + r, g) for t in range(STEPS) for g in range(3)], axis=0
        ).astype(BF16)
        live = iota((96, 512), 1) + seq * 512 < len_ref[r]
        out, lse = softmax_parts(queries, keys, values, live)
        for t, (first, second) in enumerate(message_tiles(out, lse, 12)):
            out_ref[REQS * t + r, 0:8, :] = first
            out_ref[REQS * t + r, 8:16, :] = second
        return carry

    lax.fori_loop(0, REQS, body, 0)


def attend(page_table, cache_len, queries, new_key_value, cache):
    smem = pl.BlockSpec(memory_space=pltpu.SMEM)
    vmem = pl.BlockSpec(memory_space=pltpu.VMEM)
    return pl.pallas_call(
        attend_kernel,
        out_shape=jax.ShapeDtypeStruct((N_SEQ + 1, 16, 128), F32),
        in_specs=[smem, smem, vmem, vmem, pl.BlockSpec(memory_space=pl.ANY)],
        out_specs=vmem,
        scratch_shapes=[
            VMEM((REQS, 8, 64, 2, 512), BF16),
            VMEM((TOKENS, D), F32),
            VMEM((2, 16, 512), F32),
            pltpu.SemaphoreType.DMA((REQS, 8)),
        ],
        compiler_params=pltpu.CompilerParams(vmem_limit_bytes=40 << 20),
        name="attend",
    )(page_table, cache_len, queries, new_key_value, cache)


def unit_home(u):
    return lax.div(8 * u, 5)


def layer_kernel(
    msg_ref, wo_ref, res_ref, gain_ref, wr_ref, wgu_ref, wd_ref, routes_ref, out_ref,
    flip, recv1, send2, recv2, attf, wstage, wbuf, mstage, mbuf, xstage, xbuf, x4, xt,
    w_t, r_t, ystage, ybuf, zstage, zbuf, hid, send_sems, recv_sems,
):
    me = lax.axis_index("seq")
    ex = lax.axis_index("exp")
    unit = lax.div(5 * me + 7, 8)
    working = (unit < UNITS) & (unit_home(unit) == me)
    unit_safe = jnp.minimum(unit, UNITS - 1)

    def seq_peer(i):
        return lax.rem(me + i, N_SEQ)

    def exp_peer(i):
        return lax.rem(ex + i, N_EXP)

    def push(src, dst, phase, seq=None, exp=None):
        target = (me if seq is None else seq, ex if exp is None else exp)
        pltpu.make_async_remote_copy(
            src_ref=src, dst_ref=dst, send_sem=send_sems.at[phase], recv_sem=recv_sems.at[phase],
            device_id=target, device_id_type=MESH,
        ).start()

    def drain(sems, phase, ref):
        pltpu.make_async_copy(ref, ref, sems.at[phase]).wait()

    barrier = pltpu.get_barrier_semaphore()

    def greet_seq(i, c):
        pl.semaphore_signal(barrier, inc=1, device_id=(seq_peer(i), ex), device_id_type=MESH)
        return c

    def greet_exp(i, c):
        pl.semaphore_signal(barrier, inc=1, device_id=(me, exp_peer(i)), device_id_type=MESH)
        return c

    lax.fori_loop(1, N_SEQ, greet_seq, 0)
    lax.fori_loop(1, N_EXP, greet_exp, 0)

    flip[...] = jnp.zeros_like(flip)
    flip[0:TOKENS, 0:SLICE] = res_ref[...].reshape(TOKENS, SLICE).astype(F32)
    flip[TOKENS : TOKENS + 1, 0:SLICE] = gain_ref[...]
    flip[40:80, 0:SLICE] = wr_ref[...].astype(F32)
    flip[0:TOKENS, 64:72] = routes_ref[...].reshape(TOKENS, 8).astype(F32)
    turned = flip[...].T
    top = turned[0:SLICE]
    lane48 = iota((SLICE, 128), 1)
    residual = top[:, 0:TOKENS]
    gain = top[:, TOKENS : TOKENS + 1]
    inv_gain = 1.0 / (gain * gain)
    inv_high = inv_gain.astype(BF16).astype(F32)
    router = pltpu.roll(top, 88, 1)
    router = jnp.where(lane48 == 40, inv_high, jnp.where(lane48 == 41, inv_gain - inv_high, router))
    router = jnp.where(lane48 < 42, router, 0.0).astype(BF16)
    expert_row = iota((SLICE, 128), 0).astype(F32)
    chosen = jnp.zeros((SLICE, 128), F32)
    for k in range(8):
        chosen = jnp.where(expert_row == turned[64 + k : 65 + k, :], 1.0, chosen)
    mstage[...] = chosen.astype(BF16)
    mbuf[ex] = chosen.astype(BF16)

    for j in range(EXPERTS_LOCAL):
        for c in range(4):
            cols = slice(128 * c, 128 * c + 128)
            wstage[4 * j + c, :, 0:128] = wgu_ref[j, :, 0, cols]
            wstage[4 * j + c, :, 128:256] = wgu_ref[j, :, 1, cols]
            wstage[4 * j + c, :, 256:384] = wd_ref[j, :, cols]
            wstage[4 * j + c, :, 384:512] = router
    recv1[me] = msg_ref[me]

    pl.semaphore_wait(barrier, N_SEQ + N_EXP - 2)

    def send1(i, c):
        d = seq_peer(i)
        push(msg_ref.at[d], recv1.at[me], 0, seq=d)
        return c

    lax.fori_loop(1, N_SEQ, send1, 0)

    def send_mask(i, c):
        push(mstage, mbuf.at[ex], 1, exp=exp_peer(i))
        return c

    lax.fori_loop(1, N_EXP, send_mask, 0)

    def send_weights(i, c):
        u = lax.rem(unit_safe + i, UNITS)
        d = unit_home(u)

        @pl.when(d != me)
        def _():
            push(wstage.at[u], wbuf.at[me], 2, seq=d)

        return c

    lax.fori_loop(0, UNITS, send_weights, 0)

    @pl.when(working)
    def _():
        wbuf[me] = wstage[unit_safe]

    drain(recv_sems, 0, recv1.at[pl.ds(0, N_SEQ - 1)])
    head = iota((8, 128), 0)
    lane = iota((8, 128), 1)
    odd = head % 2 == 1
    half = lane // 64 == head % 2

    def stat_of(second):
        return jnp.where(odd, second, pltpu.roll(second, 64, 1))

    fresh_stat = stat_of(msg_ref[N_SEQ, 8:16, :])
    largest = lax.fori_loop(
        0, N_SEQ, lambda s, m: jnp.maximum(m, stat_of(recv1[s, 8:16, :])), fresh_stat, unroll=8
    )

    def add_part(first, second, carry):
        total, acc1, acc2 = carry
        w = jnp.exp(stat_of(second) - largest)
        w1 = jnp.where(half, w[:, 0:1], w[:, 1:2])
        return total + w, acc1 + w1 * first, acc2 + w[:, 2:3] * second

    zero = jnp.zeros((8, 128), F32)
    carry = add_part(msg_ref[N_SEQ, 0:8, :], msg_ref[N_SEQ, 8:16, :], (zero, zero, zero))
    total, acc1, acc2 = lax.fori_loop(
        0, N_SEQ, lambda s, c: add_part(recv1[s, 0:8, :], recv1[s, 8:16, :], c), carry, unroll=8
    )
    att1 = acc1 / jnp.where(half, total[:, 0:1], total[:, 1:2])
    att2 = jnp.where(half, acc2 / total[:, 2:3], 0.0)
    token = jnp.concatenate([att1, att2], axis=0).astype(BF16)
    send2[...] = token
    recv2[me] = token

    def send_token(i, c):
        push(send2, recv2.at[me], 3, seq=seq_peer(i))
        return c

    lax.fori_loop(1, N_SEQ, send_token, 0)

    low = iota((SLICE, 128), 1) < 64

    def wo_tile(i):
        return wo_ref[:, 128 * i : 128 * i + 128].astype(F32)

    tiles = []
    for k in range(8):
        if k % 2 == 0:
            tiles.append(wo_tile(3 * k // 2))
        else:
            tiles.append(jnp.where(low, wo_tile((3 * k + 1) // 2), wo_tile((3 * k - 1) // 2)))
    for k in range(8):
        tiles.append(wo_tile((3 * k + 2) // 2))
    wo = jnp.concatenate(tiles, axis=1).astype(BF16)

    drain(recv_sems, 3, recv2.at[pl.ds(0, N_SEQ - 1)])
    attf[...] = recv2[...].astype(F32).reshape(N_SEQ * 16, 128)
    att = jnp.concatenate([attf[pl.ds(j, N_SEQ, stride=16), :] for j in range(16)], axis=1).astype(BF16)
    hidden = residual + nt_dot(wo, att)
    hid[...] = hidden
    x_own = (hidden * gain).astype(BF16)
    xstage[...] = jnp.zeros_like(xstage)
    xstage[:, 0:TOKENS] = x_own
    xbuf[ex] = xstage[...]

    def send_x(i, c):
        push(xstage, xbuf.at[ex], 4, exp=exp_peer(i))
        return c

    lax.fori_loop(1, N_EXP, send_x, 0)

    def join(ref):
        halves = []
        for h in range(2):
            joined = ref[4 * h].astype(F32)
            for i in range(1, 4):
                part = pltpu.roll(ref[4 * h + i].astype(F32), 32 * i, 1)
                joined = jnp.where(lane48 // 32 == i, part, joined)
            halves.append(joined)
        return jnp.concatenate(halves, axis=1)

    drain(recv_sems, 4, xbuf.at[pl.ds(0, N_EXP - 1)])
    x4[...] = join(xbuf).astype(BF16)

    def send_x4(i, c):
        d = unit_home(lax.rem(unit_safe + i, UNITS))

        @pl.when(d != me)
        def _():
            push(x4, xt.at[me], 5, seq=d)

        return c

    lax.fori_loop(0, UNITS, send_x4, 0)
    drain(recv_sems, 1, mbuf.at[pl.ds(0, N_EXP - 1)])

    @pl.when(working)
    def _():
        xt[me] = x4[...]
        drain(recv_sems, 2, wbuf.at[pl.ds(0, N_SEQ - 1)])
        w_t[...] = wbuf[:, :, 0:256].reshape(D, 256).T
        r_t[...] = wbuf[:, :, 384:512].reshape(D, 128).T
        mask = join(mbuf)
        drain(recv_sems, 5, xt.at[pl.ds(0, N_SEQ - 1)])
        x_all = xt[...].reshape(D, ALL_TOKENS)
        x_f32 = x_all.astype(F32)
        pre = nn_dot(w_t[...], x_all)
        small = nn_dot(r_t[0:SLICE, :], x_all)
        squares = nn_dot(r_t[40:48, :], (x_f32 * x_f32).astype(BF16))
        inv_rms = lax.rsqrt((squares[0:1] + squares[1:2]) / D + 1e-6)
        logits = small * inv_rms
        powers = jnp.where(mask > 0.5, jnp.exp(logits), 0.0)
        mine = iota((SLICE, ALL_TOKENS), 0) == ex * EXPERTS_LOCAL + lax.div(unit_safe, 4)
        gate_weight = jnp.sum(jnp.where(mine, powers, 0.0), axis=0, keepdims=True) / jnp.sum(
            powers, axis=0, keepdims=True
        )
        gate = pre[0:128] * inv_rms
        up = pre[128:256] * inv_rms
        inner = (gate / (1.0 + jnp.exp(-gate)) * up * gate_weight).astype(BF16)

        def send_y(i, c):
            d = seq_peer(i)
            ystage[d] = nn_dot(wbuf[d, :, 256:384], inner).astype(BF16)
            push(ystage.at[d], ybuf.at[unit_safe], 6, seq=d)
            return c

        lax.fori_loop(1, N_SEQ, send_y, 0)
        ybuf[unit_safe] = nn_dot(wbuf[me, :, 256:384], inner).astype(BF16)
        drain(recv_sems, 6, ybuf.at[pl.ds(0, UNITS - 1)])

    @pl.when(jnp.logical_not(working))
    def _():
        drain(recv_sems, 6, ybuf)

    summed = lax.fori_loop(
        0, UNITS, lambda u, s: s + ybuf[u].astype(F32), jnp.zeros((SLICE, ALL_TOKENS), F32), unroll=4
    )
    for e in range(N_EXP):
        part = summed[:, 128 * (e // 4) : 128 * (e // 4) + 128]
        if e % 4:
            part = pltpu.roll(part, 128 - 32 * (e % 4), 1)
        zstage[e] = part.astype(BF16)
    zbuf[ex] = zstage[ex]

    def send_z(i, c):
        e = exp_peer(i)
        push(zstage.at[e], zbuf.at[ex], 7, exp=e)
        return c

    lax.fori_loop(1, N_EXP, send_z, 0)
    drain(recv_sems, 7, zbuf.at[pl.ds(0, N_EXP - 1)])
    moe = jnp.sum(zbuf[...].astype(F32), axis=0)
    flip[0:SLICE, :] = moe
    flip[0:SLICE, 0:TOKENS] = moe[:, 0:TOKENS] + hid[...]
    out = flip[...].T
    out_ref[...] = out[0:TOKENS, 0:SLICE].reshape(STEPS, REQS, SLICE).astype(BF16)

    drain(send_sems, 0, recv1.at[pl.ds(0, N_SEQ - 1)])
    drain(send_sems, 1, mbuf.at[pl.ds(0, N_EXP - 1)])
    drain(send_sems, 3, recv2.at[pl.ds(0, N_SEQ - 1)])
    drain(send_sems, 4, xbuf.at[pl.ds(0, N_EXP - 1)])
    drain(send_sems, 7, zbuf.at[pl.ds(0, N_EXP - 1)])

    @pl.when(working)
    def _():
        drain(send_sems, 2, wbuf.at[pl.ds(0, UNITS - 1)])
        drain(send_sems, 5, xt.at[pl.ds(0, UNITS - 1)])
        drain(send_sems, 6, xt.at[pl.ds(0, N_SEQ - 1)])

    @pl.when(jnp.logical_not(working))
    def _():
        drain(send_sems, 2, wbuf.at[pl.ds(0, UNITS)])
        drain(send_sems, 5, xt.at[pl.ds(0, UNITS)])


def layer(messages, wo, residual, gain, router, gate_up, down, routes):
    vmem = pl.BlockSpec(memory_space=pltpu.VMEM)
    return pl.pallas_call(
        layer_kernel,
        out_shape=jax.ShapeDtypeStruct((STEPS, REQS, SLICE), BF16),
        in_specs=[vmem] * 8,
        out_specs=vmem,
        scratch_shapes=[
            VMEM((128, 128), F32),
            VMEM((N_SEQ, 16, 128), F32),
            VMEM((16, 128), BF16),
            VMEM((N_SEQ, 16, 128), BF16),
            VMEM((N_SEQ * 16, 128), F32),
            VMEM((UNITS, SLICE, 512), BF16),
            VMEM((N_SEQ, SLICE, 512), BF16),
            VMEM((SLICE, 128), BF16),
            VMEM((N_EXP, SLICE, 128), BF16),
            VMEM((SLICE, 128), BF16),
            VMEM((N_EXP, SLICE, 128), BF16),
            VMEM((SLICE, ALL_TOKENS), BF16),
            VMEM((N_SEQ, SLICE, ALL_TOKENS), BF16),
            VMEM((256, D), BF16),
            VMEM((128, D), BF16),
            VMEM((N_SEQ, SLICE, ALL_TOKENS), BF16),
            VMEM((UNITS, SLICE, ALL_TOKENS), BF16),
            VMEM((N_EXP, SLICE, 128), BF16),
            VMEM((N_EXP, SLICE, 128), BF16),
            VMEM((SLICE, TOKENS), F32),
            pltpu.SemaphoreType.DMA((8,)),
            pltpu.SemaphoreType.DMA((8,)),
        ],
        compiler_params=pltpu.CompilerParams(
            collective_id=0, has_side_effects=True, vmem_limit_bytes=40 << 20
        ),
        name="layer",
    )(messages, wo, residual, gain, router, gate_up, down, routes)


def local(
    queries,
    new_key_value,
    key_value_cache,
    page_table,
    cache_len,
    routes,
    residual,
    w_out,
    norm_gain,
    w_router,
    w_gate_up,
    w_down,
):
    cache = key_value_cache.reshape(64, 64, 2, 512)
    messages = attend(page_table, cache_len, queries, new_key_value, cache)
    return layer(
        messages, w_out.T, residual, norm_gain.reshape(1, SLICE), w_router.T, w_gate_up, w_down, routes
    )


def solution(mesh):
    in_specs = (
        P(None, "exp", None),
        P(None, "exp", None, None),
        P("exp", "seq", None, None, None),
        P("exp", "seq"),
        P("exp"),
        P(None, "exp", None),
        P(None, "exp", "seq"),
        P(None, "seq"),
        P("seq"),
        P("seq", None),
        P("exp", "seq", None, None),
        P("exp", "seq", None),
    )
    out_specs = P(None, "exp", "seq")
    return jax.shard_map(local, mesh=mesh, in_specs=in_specs, out_specs=out_specs, check_vma=False)
```

```python
import jax
import jax.numpy as jnp
from jax import lax
from jax.experimental import pallas as pl
from jax.experimental.pallas import tpu as pltpu
from jax.sharding import PartitionSpec as P

NEG = -1e30
N_SEQ = 32
N_EXP = 8
STEPS = 4
REQS = 8
TOKENS = STEPS * REQS
EXPERTS = 40
EXPERTS_LOCAL = 5
PER_BLOCK = 1
BLOCKS = 20 // PER_BLOCK
WIDTH = 128 * PER_BLOCK
TOGETHER = 2
SLOTS = 128
SLICE = 48
D = 1536
ALL_TOKENS = TOKENS * N_EXP
F32 = jnp.float32
BF16 = jnp.bfloat16
MESH = pl.DeviceIdType.MESH
VMEM = pltpu.VMEM


def iota(shape, axis):
    return lax.broadcasted_iota(jnp.int32, shape, axis)


def nt_dot(a, b):
    return lax.dot_general(a, b, (((1,), (1,)), ((), ())), preferred_element_type=F32)


def nn_dot(a, b):
    return lax.dot_general(a, b, (((1,), (0,)), ((), ())), preferred_element_type=F32)


def spread_queries(q_ref, rows_ref):
    low = iota((REQS, 128), 1) < 64
    for t in range(STEPS):
        q = q_ref[t].astype(F32) * 0.125
        tiles = [q[:, 128 * i : 128 * i + 128] for i in range(12)]
        for g in range(3):
            for pair in range(4):
                first, second = 6 * pair + g, 6 * pair + 3 + g
                if g == 1:
                    tile = jnp.where(low, tiles[second // 2], tiles[first // 2])
                    tile = pltpu.roll(tile, 64, 1)
                else:
                    tile = jnp.where(low, tiles[first // 2], tiles[second // 2])
                base = g * 512 + pair * 128
                rows_ref[REQS * t : REQS * t + REQS, base : base + 128] = tile


def block_diagonal(rows_ref, row, g):
    own = iota((8, 512), 1) // 64 == iota((8, 512), 0)
    values = rows_ref[pl.ds(row, 1), 512 * g : 512 * g + 512]
    return jnp.where(own, jnp.broadcast_to(values, (8, 512)), 0.0)


def softmax_parts(queries, keys, values, live):
    scores = jnp.where(live, nt_dot(queries, keys), NEG)
    largest = jnp.max(scores, axis=1, keepdims=True)
    weights = jnp.where(live, jnp.exp(scores - largest), 0.0)
    total = jnp.sum(weights, axis=1, keepdims=True)
    if values is None:
        acc = nn_dot(pltpu.roll(weights, 1, 1).astype(BF16), keys)
    else:
        acc = nn_dot(weights.astype(BF16), values)
    some = total > 0.0
    safe = jnp.where(some, total, 1.0)
    return acc / safe, jnp.where(some, largest + jnp.log(safe), NEG)


def message_tiles(out, lse, groups):
    out = out.reshape(groups, 8, 512)
    lse = lse.reshape(groups, 8, 1)
    head = iota((groups, 8, 128), 1)
    lane = iota((groups, 8, 128), 2)
    packed = out[:, :, 0:128]
    for j in range(1, 4):
        packed = jnp.where(head // 2 == j, out[:, :, 128 * j : 128 * j + 128], packed)
    packed = jnp.where(lane // 64 == head % 2, packed, 0.0)
    head, lane = head[0], lane[0]
    free = lane // 64 != head % 2
    place = lane % 64
    tiles = []
    for t in range(groups // 3):
        first = packed[3 * t] + pltpu.roll(packed[3 * t + 1], 64, 1)
        stat = jnp.where(place == 0, lse[3 * t], jnp.where(place == 1, lse[3 * t + 1], lse[3 * t + 2]))
        second = packed[3 * t + 2] + jnp.where(free & (place < 3), stat, 0.0)
        tiles.append((first, second))
    return tiles


def block_home(b):
    return lax.div(N_SEQ * b, BLOCKS)


def layer_kernel(
    table_ref, len_ref, q_hbm, new_hbm, kv_hbm, wo_hbm, res_hbm, gain_hbm, wr_hbm, wgu_hbm, wd_hbm, routes_hbm,
    out_ref,
    q_ref, new_ref, pages, wo_ref, res_ref, gain_ref, wr_ref, wgu_ref, wd_ref, routes_ref,
    rows, fresh, msg,
    flip, recv1, send2, recv2, attf, wstage, wbuf, mstage, mbuf, xstage, xbuf, slot, spread, xs, xt,
    w_t, r_t, ystage, ybuf, zstage, zbuf, hid, in_sems, page_sems, send_sems, recv_sems,
):
    me = lax.axis_index("seq")
    ex = lax.axis_index("exp")
    block = lax.div(BLOCKS * me + N_SEQ - 1, N_SEQ)
    working = (block < BLOCKS) & (block_home(block) == me)
    block_safe = jnp.minimum(block, BLOCKS - 1)
    expert_own = lax.div(block_safe * PER_BLOCK, 4)

    def seq_peer(i):
        return lax.rem(me + i, N_SEQ)

    def exp_peer(i):
        return lax.rem(ex + i, N_EXP)

    def push(src, dst, phase, seq=None, exp=None):
        target = (me if seq is None else seq, ex if exp is None else exp)
        pltpu.make_async_remote_copy(
            src_ref=src, dst_ref=dst, send_sem=send_sems.at[phase], recv_sem=recv_sems.at[phase],
            device_id=target, device_id_type=MESH,
        ).start()

    def drain(sems, phase, ref):
        pltpu.make_async_copy(ref, ref, sems.at[phase]).wait()

    loads = [
        pltpu.make_async_copy(src, dst, in_sems.at[i])
        for i, (src, dst) in enumerate(
            (
                (wgu_hbm, wgu_ref), (wd_hbm, wd_ref), (res_hbm, res_ref), (gain_hbm, gain_ref), (wr_hbm, wr_ref),
                (routes_hbm, routes_ref), (q_hbm, q_ref), (new_hbm, new_ref), (wo_hbm, wo_ref),
            )
        )
    ]
    for load in loads:
        load.start()
    page_loads = [
        pltpu.make_async_copy(
            kv_hbm.at[8 * i : 8 * i + 8, :, c], pages.at[c, 8 * i : 8 * i + 8], page_sems.at[4 * i + c]
        )
        for i in range(8)
        for c in range(4)
    ]
    for load in page_loads:
        load.start()

    barrier = pltpu.get_barrier_semaphore()

    def greet_seq(i, c):
        pl.semaphore_signal(barrier, inc=1, device_id=(seq_peer(i), ex), device_id_type=MESH)
        return c

    def greet_exp(i, c):
        pl.semaphore_signal(barrier, inc=1, device_id=(me, exp_peer(i)), device_id_type=MESH)
        return c

    lax.fori_loop(1, N_SEQ, greet_seq, 0)
    lax.fori_loop(1, N_EXP, greet_exp, 0)

    for load in loads[:6]:
        load.wait()
    flip[...] = jnp.zeros_like(flip)
    flip[0:TOKENS, 0:SLICE] = res_ref[...].reshape(TOKENS, SLICE).astype(F32)
    flip[TOKENS : TOKENS + 1, 0:SLICE] = gain_ref[...]
    flip[40:80, 0:SLICE] = wr_ref[...].astype(F32)
    flip[0:TOKENS, 64:72] = routes_ref[...].reshape(TOKENS, 8).astype(F32)
    turned = flip[...].T
    top = turned[0:SLICE]
    lane48 = iota((SLICE, 128), 1)
    residual = top[:, 0:TOKENS]
    gain = top[:, TOKENS : TOKENS + 1]
    inv_gain = 1.0 / (gain * gain)
    inv_high = inv_gain.astype(BF16).astype(F32)
    router = pltpu.roll(top, 88, 1)
    router = jnp.where(lane48 == 40, inv_high, jnp.where(lane48 == 41, inv_gain - inv_high, router))
    router = jnp.where(lane48 < 42, router, 0.0).astype(BF16)
    expert_row = iota((SLICE, 128), 0).astype(F32)
    chosen = jnp.zeros((SLICE, 128), F32)
    for k in range(8):
        chosen = jnp.where(expert_row == turned[64 + k : 65 + k, :], 1.0, chosen)
    mstage[...] = chosen.astype(BF16)
    mbuf[ex] = chosen.astype(BF16)

    for b in range(BLOCKS):
        for i in range(PER_BLOCK):
            j, c = divmod(b * PER_BLOCK + i, 4)
            cols = slice(128 * c, 128 * c + 128)
            at = 128 * i
            wstage[b, :, at : at + 128] = wgu_ref[j, :, 0, cols]
            wstage[b, :, WIDTH + at : WIDTH + at + 128] = wgu_ref[j, :, 1, cols]
            wstage[b, :, 2 * WIDTH + at : 2 * WIDTH + at + 128] = wd_ref[j, :, cols]
        wstage[b, :, 3 * WIDTH : 3 * WIDTH + 128] = router

    pl.semaphore_wait(barrier, N_SEQ + N_EXP - 2)

    def send_mask(i, c):
        push(mstage, mbuf.at[ex], 1, exp=exp_peer(i))
        return c

    lax.fori_loop(1, N_EXP, send_mask, 0)

    def send_weights(i, c):
        b = lax.rem(block_safe + i, BLOCKS)
        d = block_home(b)

        @pl.when(d != me)
        def _():
            push(wstage.at[b], wbuf.at[me], 2, seq=d)

        return c


    @pl.when(working)
    def _():
        wbuf[me] = wstage[block_safe]

    for load in loads[6:8]:
        load.wait()
    spread_queries(q_ref, rows)
    t_own, r_own = lax.div(me, 8), lax.rem(me, 8)
    fresh[...] = jnp.zeros_like(fresh)
    for u in range(STEPS):
        for kind in range(2):
            fresh[kind, u : u + 1, :] = new_ref[u, r_own, kind : kind + 1, :].astype(F32)
    queries = jnp.concatenate([block_diagonal(rows, me, g) for g in range(3)], axis=0).astype(BF16)
    live = iota((24, 16), 1) <= t_own
    out, lse = softmax_parts(queries, fresh[0].astype(BF16), fresh[1].astype(BF16), live)
    ((fresh_first, fresh_second),) = message_tiles(out, lse, 3)

    for load in page_loads:
        load.wait()

    def attend(r):
        both = jnp.concatenate(
            [
                jnp.concatenate([pages[c, table_ref[r, j]].reshape(128, 128) for j in range(8)], axis=0)
                for c in range(4)
            ],
            axis=1,
        )
        queries = jnp.concatenate(
            [block_diagonal(rows, REQS * t + r, g) for t in range(STEPS) for g in range(3)], axis=0
        ).astype(BF16)
        lane = iota((96, 1024), 1)
        live = (lane // 2 + me * 512 < len_ref[r]) & (lane % 2 == 0)
        out, lse = softmax_parts(queries, both, None, live)
        for t, (first, second) in enumerate(message_tiles(out, lse, 12)):
            msg[REQS * t + r, 0:8, :] = first
            msg[REQS * t + r, 8:16, :] = second

    def attend_some(step, c):
        for i in range(TOGETHER):
            attend(step * TOGETHER + i)
        for i in range(TOGETHER):
            for t in range(STEPS):
                d = REQS * t + step * TOGETHER + i

                @pl.when(d != me)
                def _():
                    push(msg.at[d], recv1.at[me], 0, seq=d)

        return c

    lax.fori_loop(0, REQS // TOGETHER, attend_some, 0)
    lax.fori_loop(0, BLOCKS, send_weights, 0)
    recv1[me] = msg[me]

    loads[8].wait()
    low = iota((SLICE, 128), 1) < 64

    def wo_tile(i):
        return wo_ref[:, 128 * i : 128 * i + 128].astype(F32)

    tiles = []
    for k in range(8):
        if k % 2 == 0:
            tiles.append(wo_tile(3 * k // 2))
        else:
            tiles.append(jnp.where(low, wo_tile((3 * k + 1) // 2), wo_tile((3 * k - 1) // 2)))
    for k in range(8):
        tiles.append(wo_tile((3 * k + 2) // 2))
    wo = jnp.concatenate(tiles, axis=1).astype(BF16)

    def join(ref):
        halves = []
        for h in range(2):
            joined = ref[4 * h].astype(F32)
            for i in range(1, 4):
                part = pltpu.roll(ref[4 * h + i].astype(F32), 32 * i, 1)
                joined = jnp.where(lane48 // 32 == i, part, joined)
            halves.append(joined)
        return jnp.concatenate(halves, axis=1)

    drain(recv_sems, 1, mbuf.at[pl.ds(0, N_EXP - 1)])
    mask = join(mbuf)
    row, col = iota((ALL_TOKENS, ALL_TOKENS), 0), iota((ALL_TOKENS, ALL_TOKENS), 1)
    earlier = jnp.where((row // 8 == col // 8) & (row < col), 1.0, 0.0).astype(BF16)
    rank = nn_dot(mask.astype(BF16), earlier)
    group = (iota((SLICE, ALL_TOKENS), 1) // 8 * 4).astype(F32)
    slot[...] = jnp.where(mask > 0.5, group + rank, -1.0)
    slot_row = iota((SLOTS, ALL_TOKENS), 0).astype(F32)
    for j in range(EXPERTS_LOCAL):
        slots = slot[pl.ds(ex * EXPERTS_LOCAL + j, 1), :]
        spread[j] = jnp.where(slot_row == slots, 1.0, 0.0).astype(BF16)

    drain(recv_sems, 0, recv1.at[pl.ds(0, N_SEQ - 1)])
    head = iota((8, 128), 0)
    lane = iota((8, 128), 1)
    odd = head % 2 == 1
    half = lane // 64 == head % 2

    def stat_of(second):
        return jnp.where(odd, second, pltpu.roll(second, 64, 1))

    largest = lax.fori_loop(
        0, N_SEQ, lambda s, m: jnp.maximum(m, stat_of(recv1[s, 8:16, :])), stat_of(fresh_second), unroll=8
    )

    def add_part(first, second, carry):
        total, acc1, acc2 = carry
        w = jnp.exp(stat_of(second) - largest)
        w1 = jnp.where(half, w[:, 0:1], w[:, 1:2])
        return total + w, acc1 + w1 * first, acc2 + w[:, 2:3] * second

    zero = jnp.zeros((8, 128), F32)
    carry = add_part(fresh_first, fresh_second, (zero, zero, zero))
    total, acc1, acc2 = lax.fori_loop(
        0, N_SEQ, lambda s, c: add_part(recv1[s, 0:8, :], recv1[s, 8:16, :], c), carry, unroll=8
    )
    att1 = acc1 / jnp.where(half, total[:, 0:1], total[:, 1:2])
    att2 = jnp.where(half, acc2 / total[:, 2:3], 0.0)
    token = jnp.concatenate([att1, att2], axis=0).astype(BF16)
    send2[...] = token
    recv2[me] = token

    def send_token(i, c):
        push(send2, recv2.at[me], 3, seq=seq_peer(i))
        return c

    lax.fori_loop(1, N_SEQ, send_token, 0)

    drain(recv_sems, 3, recv2.at[pl.ds(0, N_SEQ - 1)])
    attf[...] = recv2[...].astype(F32).reshape(N_SEQ * 16, 128)
    att = jnp.concatenate([attf[pl.ds(j, N_SEQ, stride=16), :] for j in range(16)], axis=1).astype(BF16)
    hidden = residual + nt_dot(wo, att)
    hid[...] = hidden
    xstage[...] = jnp.zeros_like(xstage)
    xstage[:, 0:TOKENS] = (hidden * gain).astype(BF16)
    xbuf[ex] = xstage[...]

    def send_x(i, c):
        push(xstage, xbuf.at[ex], 4, exp=exp_peer(i))
        return c

    lax.fori_loop(1, N_EXP, send_x, 0)

    drain(recv_sems, 4, xbuf.at[pl.ds(0, N_EXP - 1)])
    x4 = join(xbuf).astype(BF16)
    for j in range(EXPERTS_LOCAL):
        xs[j] = nt_dot(x4, spread[j]).astype(BF16)

    def send_slots(i, c):
        b = lax.rem(block_safe + i, BLOCKS)
        d = block_home(b)

        @pl.when(d != me)
        def _():
            push(xs.at[lax.div(b * PER_BLOCK, 4)], xt.at[me], 5, seq=d)

        return c

    lax.fori_loop(0, BLOCKS, send_slots, 0)

    @pl.when(working)
    def _():
        xt[me] = xs[expert_own]
        drain(recv_sems, 2, wbuf.at[pl.ds(0, N_SEQ - 1)])
        w_t[...] = wbuf[:, :, 0 : 2 * WIDTH].reshape(D, 2 * WIDTH).T
        r_t[...] = wbuf[:, :, 3 * WIDTH : 3 * WIDTH + 128].reshape(D, 128).T
        slot_mask = nt_dot(mask.astype(BF16), spread[expert_own])
        drain(recv_sems, 5, xt.at[pl.ds(0, N_SEQ - 1)])
        x_all = xt[...].reshape(D, SLOTS)
        x_f32 = x_all.astype(F32)
        pre = nn_dot(w_t[...], x_all)
        small = nn_dot(r_t[0:SLICE, :], x_all)
        squares = nn_dot(r_t[40:48, :], (x_f32 * x_f32).astype(BF16))
        inv_rms = lax.rsqrt((squares[0:1] + squares[1:2]) / D + 1e-6)
        powers = jnp.where(slot_mask > 0.5, jnp.exp(small * inv_rms), 0.0)
        mine = iota((SLICE, SLOTS), 0) == ex * EXPERTS_LOCAL + expert_own
        whole = jnp.sum(powers, axis=0, keepdims=True)
        gate_weight = jnp.sum(jnp.where(mine, powers, 0.0), axis=0, keepdims=True) / jnp.where(
            whole > 0.0, whole, 1.0
        )
        gate = pre[0:WIDTH] * inv_rms
        up = pre[WIDTH : 2 * WIDTH] * inv_rms
        inner = (gate / (1.0 + jnp.exp(-gate)) * up * gate_weight).astype(BF16)

        def send_y(i, c):
            d = seq_peer(i)
            ystage[d] = nn_dot(wbuf[d, :, 2 * WIDTH : 3 * WIDTH], inner).astype(BF16)
            push(ystage.at[d], ybuf.at[block_safe], 6, seq=d)
            return c

        lax.fori_loop(1, N_SEQ, send_y, 0)
        ybuf[block_safe] = nn_dot(wbuf[me, :, 2 * WIDTH : 3 * WIDTH], inner).astype(BF16)
        drain(recv_sems, 6, ybuf.at[pl.ds(0, BLOCKS - 1)])

    @pl.when(jnp.logical_not(working))
    def _():
        drain(recv_sems, 6, ybuf)

    per_expert = BLOCKS // EXPERTS_LOCAL
    summed = jnp.zeros((SLICE, ALL_TOKENS), F32)
    for j in range(EXPERTS_LOCAL):
        part = ybuf[per_expert * j].astype(F32)
        for i in range(1, per_expert):
            part = part + ybuf[per_expert * j + i].astype(F32)
        summed = summed + nn_dot(part.astype(BF16), spread[j])
    for e in range(N_EXP):
        part = summed[:, 128 * (e // 4) : 128 * (e // 4) + 128]
        if e % 4:
            part = pltpu.roll(part, 128 - 32 * (e % 4), 1)
        zstage[e] = part.astype(BF16)
    zbuf[ex] = zstage[ex]

    def send_z(i, c):
        e = exp_peer(i)
        push(zstage.at[e], zbuf.at[ex], 7, exp=e)
        return c

    lax.fori_loop(1, N_EXP, send_z, 0)
    drain(recv_sems, 7, zbuf.at[pl.ds(0, N_EXP - 1)])
    moe = jnp.sum(zbuf[...].astype(F32), axis=0)
    flip[0:SLICE, :] = moe
    flip[0:SLICE, 0:TOKENS] = moe[:, 0:TOKENS] + hid[...]
    out = flip[...].T
    out_ref[...] = out[0:TOKENS, 0:SLICE].reshape(STEPS, REQS, SLICE).astype(BF16)

    drain(send_sems, 0, recv1.at[pl.ds(0, N_SEQ - 1)])
    drain(send_sems, 1, mbuf.at[pl.ds(0, N_EXP - 1)])
    drain(send_sems, 3, recv2.at[pl.ds(0, N_SEQ - 1)])
    drain(send_sems, 4, xbuf.at[pl.ds(0, N_EXP - 1)])
    drain(send_sems, 7, zbuf.at[pl.ds(0, N_EXP - 1)])

    @pl.when(working)
    def _():
        drain(send_sems, 2, wbuf.at[pl.ds(0, BLOCKS - 1)])
        drain(send_sems, 5, xt.at[pl.ds(0, BLOCKS - 1)])
        drain(send_sems, 6, xt.at[pl.ds(0, N_SEQ - 1)])

    @pl.when(jnp.logical_not(working))
    def _():
        drain(send_sems, 2, wbuf.at[pl.ds(0, BLOCKS)])
        drain(send_sems, 5, xt.at[pl.ds(0, BLOCKS)])


def layer(page_table, cache_len, *arrays):
    smem = pl.BlockSpec(memory_space=pltpu.SMEM)
    hbm = pl.BlockSpec(memory_space=pltpu.HBM)
    return pl.pallas_call(
        layer_kernel,
        out_shape=jax.ShapeDtypeStruct((STEPS, REQS, SLICE), BF16),
        in_specs=[smem, smem] + [hbm] * 10,
        out_specs=pl.BlockSpec(memory_space=pltpu.VMEM),
        scratch_shapes=[
            VMEM((STEPS, REQS, D), BF16),
            VMEM((STEPS, REQS, 2, 512), BF16),
            VMEM((4, 64, 64, 2, 128), BF16),
            VMEM((SLICE, D), BF16),
            VMEM((STEPS, REQS, SLICE), BF16),
            VMEM((1, SLICE), F32),
            VMEM((EXPERTS, SLICE), BF16),
            VMEM((EXPERTS_LOCAL, SLICE, 2, 512), BF16),
            VMEM((EXPERTS_LOCAL, SLICE, 512), BF16),
            VMEM((STEPS, REQS, 8), jnp.int32),
            VMEM((TOKENS, D), F32),
            VMEM((2, 16, 512), F32),
            VMEM((N_SEQ, 16, 128), F32),
            VMEM((128, 128), F32),
            VMEM((N_SEQ, 16, 128), F32),
            VMEM((16, 128), BF16),
            VMEM((N_SEQ, 16, 128), BF16),
            VMEM((N_SEQ * 16, 128), F32),
            VMEM((BLOCKS, SLICE, 3 * WIDTH + 128), BF16),
            VMEM((N_SEQ, SLICE, 3 * WIDTH + 128), BF16),
            VMEM((SLICE, 128), BF16),
            VMEM((N_EXP, SLICE, 128), BF16),
            VMEM((SLICE, 128), BF16),
            VMEM((N_EXP, SLICE, 128), BF16),
            VMEM((SLICE, ALL_TOKENS), F32),
            VMEM((EXPERTS_LOCAL, SLOTS, ALL_TOKENS), BF16),
            VMEM((EXPERTS_LOCAL, SLICE, SLOTS), BF16),
            VMEM((N_SEQ, SLICE, SLOTS), BF16),
            VMEM((2 * WIDTH, D), BF16),
            VMEM((128, D), BF16),
            VMEM((N_SEQ, SLICE, SLOTS), BF16),
            VMEM((BLOCKS, SLICE, SLOTS), BF16),
            VMEM((N_EXP, SLICE, 128), BF16),
            VMEM((N_EXP, SLICE, 128), BF16),
            VMEM((SLICE, TOKENS), F32),
            pltpu.SemaphoreType.DMA((9,)),
            pltpu.SemaphoreType.DMA((32,)),
            pltpu.SemaphoreType.DMA((8,)),
            pltpu.SemaphoreType.DMA((8,)),
        ],
        compiler_params=pltpu.CompilerParams(
            collective_id=0, has_side_effects=True, vmem_limit_bytes=60 << 20
        ),
        name="layer",
    )(page_table, cache_len, *arrays)


def local(
    queries,
    new_key_value,
    key_value_cache,
    page_table,
    cache_len,
    routes,
    residual,
    w_out,
    norm_gain,
    w_router,
    w_gate_up,
    w_down,
):
    cache = key_value_cache.reshape(64, 64, 2, 4, 128).transpose(0, 1, 3, 2, 4)
    return layer(
        page_table, cache_len, queries, new_key_value, cache, w_out.T, residual, norm_gain.reshape(1, SLICE),
        w_router.T, w_gate_up, w_down, routes,
    )


def solution(mesh):
    in_specs = (
        P(None, "exp", None),
        P(None, "exp", None, None),
        P("exp", "seq", None, None, None),
        P("exp", "seq"),
        P("exp"),
        P(None, "exp", None),
        P(None, "exp", "seq"),
        P(None, "seq"),
        P("seq"),
        P("seq", None),
        P("exp", "seq", None, None),
        P("exp", "seq", None),
    )
    out_specs = P(None, "exp", "seq")
    return jax.shard_map(local, mesh=mesh, in_specs=in_specs, out_specs=out_specs, check_vma=False)
```

```python
import jax
import jax.numpy as jnp
from jax import lax
from jax.experimental import pallas as pl
from jax.experimental.pallas import tpu as pltpu
from jax.sharding import PartitionSpec as P

NEG = -1e30
N_SEQ = 32
N_EXP = 8
STEPS = 4
REQS = 8
TOKENS = STEPS * REQS
EXPERTS = 40
EXPERTS_LOCAL = 5
OWN_SLOTS = 16
LOCAL_SLOTS = EXPERTS_LOCAL * OWN_SLOTS
TOGETHER = 2
SLOTS = 128
SLICE = 48
N_X = 4
N_Z = 8
PLANE = N_X * SLICE
D = 1536
ALL_TOKENS = TOKENS * N_EXP
F32 = jnp.float32
BF16 = jnp.bfloat16
MESH = pl.DeviceIdType.MESH
VMEM = pltpu.VMEM


def iota(shape, axis):
    return lax.broadcasted_iota(jnp.int32, shape, axis)


def nt_dot(a, b):
    return lax.dot_general(a, b, (((1,), (1,)), ((), ())), preferred_element_type=F32)


def nn_dot(a, b):
    return lax.dot_general(a, b, (((1,), (0,)), ((), ())), preferred_element_type=F32)


def spread_queries(q_ref, rows_ref):
    low = iota((REQS, 128), 1) < 64
    for t in range(STEPS):
        q = q_ref[t].astype(F32) * 0.125
        tiles = [q[:, 128 * i : 128 * i + 128] for i in range(12)]
        for g in range(3):
            for pair in range(4):
                first, second = 6 * pair + g, 6 * pair + 3 + g
                if g == 1:
                    tile = jnp.where(low, tiles[second // 2], tiles[first // 2])
                    tile = pltpu.roll(tile, 64, 1)
                else:
                    tile = jnp.where(low, tiles[first // 2], tiles[second // 2])
                base = g * 512 + pair * 128
                rows_ref[REQS * t : REQS * t + REQS, base : base + 128] = tile


def block_diagonal(rows_ref, row, g):
    own = iota((8, 512), 1) // 64 == iota((8, 512), 0)
    values = rows_ref[pl.ds(row, 1), 512 * g : 512 * g + 512]
    return jnp.where(own, jnp.broadcast_to(values, (8, 512)), 0.0)


def softmax_parts(queries, keys, values, live):
    scores = jnp.where(live, nt_dot(queries, keys), NEG)
    largest = jnp.max(scores, axis=1, keepdims=True)
    weights = jnp.where(live, jnp.exp(scores - largest), 0.0)
    total = jnp.sum(weights, axis=1, keepdims=True)
    if values is None:
        acc = nn_dot(pltpu.roll(weights, 1, 1).astype(BF16), keys)
    else:
        acc = nn_dot(weights.astype(BF16), values)
    some = total > 0.0
    safe = jnp.where(some, total, 1.0)
    return acc / safe, jnp.where(some, largest + jnp.log(safe), NEG)


def message_tiles(out, lse, groups):
    out = out.reshape(groups, 8, 512)
    lse = lse.reshape(groups, 8, 1)
    head = iota((groups, 8, 128), 1)
    lane = iota((groups, 8, 128), 2)
    packed = out[:, :, 0:128]
    for j in range(1, 4):
        packed = jnp.where(head // 2 == j, out[:, :, 128 * j : 128 * j + 128], packed)
    packed = jnp.where(lane // 64 == head % 2, packed, 0.0)
    head, lane = head[0], lane[0]
    free = lane // 64 != head % 2
    place = lane % 64
    tiles = []
    for t in range(groups // 3):
        first = packed[3 * t] + pltpu.roll(packed[3 * t + 1], 64, 1)
        stat = jnp.where(place == 0, lse[3 * t], jnp.where(place == 1, lse[3 * t + 1], lse[3 * t + 2]))
        second = packed[3 * t + 2] + jnp.where(free & (place < 3), stat, 0.0)
        tiles.append((first, second))
    return tiles


def layer_kernel(
    table_ref, len_ref, q_hbm, new_hbm, kv_hbm, wo_hbm, res_hbm, gain_hbm, wr_hbm, wgu_hbm, wd_hbm, routes_hbm,
    out_ref,
    q_ref, new_ref, pages, wo_ref, res_ref, gain_ref, wr_ref, wgu_ref, wd_ref, routes_ref,
    rows, fresh, msg, flip, recv1, send2, recv2, attf, wstage, wbuf, rbuf, mstage, mbuf, xstage, xbuf,
    slot, slot_z, spread, spread_t, gather_z, mask_z, down, x4, xq, pstage, pbuf, istage, ibuf,
    ystage, ybuf, zstage, zbuf, hid, in_sems, page_sems, send_sems, recv_sems,
):
    me = lax.axis_index("seq")
    ex = lax.axis_index("exp")
    x_own, z_own = lax.div(me, N_Z), lax.rem(me, N_Z)

    def seq_peer(i):
        return lax.rem(me + i, N_SEQ)

    def exp_peer(i):
        return lax.rem(ex + i, N_EXP)

    def x_peer(i):
        return lax.rem(x_own + i, N_X)

    def z_peer(i):
        return lax.rem(z_own + i, N_Z)

    def push(src, dst, phase, seq=None, exp=None):
        target = (me if seq is None else seq, ex if exp is None else exp)
        pltpu.make_async_remote_copy(
            src_ref=src, dst_ref=dst, send_sem=send_sems.at[phase], recv_sem=recv_sems.at[phase],
            device_id=target, device_id_type=MESH,
        ).start()

    def drain(sems, phase, ref):
        pltpu.make_async_copy(ref, ref, sems.at[phase]).wait()

    loads = [
        pltpu.make_async_copy(src, dst, in_sems.at[i])
        for i, (src, dst) in enumerate(
            (
                (wgu_hbm, wgu_ref), (wd_hbm, wd_ref), (res_hbm, res_ref), (gain_hbm, gain_ref), (wr_hbm, wr_ref),
                (routes_hbm, routes_ref), (q_hbm, q_ref), (new_hbm, new_ref), (wo_hbm, wo_ref),
            )
        )
    ]
    for load in loads:
        load.start()
    page_loads = [
        pltpu.make_async_copy(
            kv_hbm.at[8 * i : 8 * i + 8, :, c], pages.at[c, 8 * i : 8 * i + 8], page_sems.at[4 * i + c]
        )
        for i in range(8)
        for c in range(4)
    ]
    for load in page_loads:
        load.start()

    barrier = pltpu.get_barrier_semaphore()

    def greet_seq(i, c):
        pl.semaphore_signal(barrier, inc=1, device_id=(seq_peer(i), ex), device_id_type=MESH)
        return c

    def greet_exp(i, c):
        pl.semaphore_signal(barrier, inc=1, device_id=(me, exp_peer(i)), device_id_type=MESH)
        return c

    lax.fori_loop(1, N_SEQ, greet_seq, 0)
    lax.fori_loop(1, N_EXP, greet_exp, 0)

    for load in loads[:6]:
        load.wait()
    flip[...] = jnp.zeros_like(flip)
    flip[0:TOKENS, 0:SLICE] = res_ref[...].reshape(TOKENS, SLICE).astype(F32)
    flip[TOKENS : TOKENS + 1, 0:SLICE] = gain_ref[...]
    flip[40:80, 0:SLICE] = wr_ref[...].astype(F32)
    flip[0:TOKENS, 64:72] = routes_ref[...].reshape(TOKENS, 8).astype(F32)
    turned = flip[...].T
    top = turned[0:SLICE]
    lane48 = iota((SLICE, 128), 1)
    residual = top[:, 0:TOKENS]
    gain = top[:, TOKENS : TOKENS + 1]
    inv_gain = 1.0 / (gain * gain)
    inv_high = inv_gain.astype(BF16).astype(F32)
    router = pltpu.roll(top, 88, 1)
    router = jnp.where(lane48 == 40, inv_high, jnp.where(lane48 == 41, inv_gain - inv_high, router))
    router = jnp.where(lane48 < 42, router, 0.0).astype(BF16)
    expert_row = iota((SLICE, 128), 0).astype(F32)
    chosen = jnp.zeros((SLICE, 128), F32)
    for k in range(8):
        chosen = jnp.where(expert_row == turned[64 + k : 65 + k, :], 1.0, chosen)
    mstage[...] = chosen.astype(BF16)
    mbuf[ex] = chosen.astype(BF16)

    for j in range(EXPERTS_LOCAL):
        for c in range(N_X):
            cols = slice(128 * c, 128 * c + 128)
            wstage[c, j, :, 0:128] = wgu_ref[j, :, 0, cols]
            wstage[c, j, :, 128:256] = wgu_ref[j, :, 1, cols]
            wstage[c, j, :, 256:384] = wd_ref[j, :, cols]
    wbuf[x_own] = wstage[x_own]
    rbuf[x_own] = router

    def send_mask(i, c):
        push(mstage, mbuf.at[ex], 1, exp=exp_peer(i))
        return c

    def send_weights(i, c):
        x = x_peer(i)
        push(wstage.at[x], wbuf.at[x_own], 2, seq=x * N_Z + z_own)
        push(rbuf.at[x_own], rbuf.at[x_own], 10, seq=x * N_Z + z_own)
        return c

    for load in loads[6:8]:
        load.wait()
    spread_queries(q_ref, rows)
    t_own, r_own = lax.div(me, 8), lax.rem(me, 8)
    fresh[...] = jnp.zeros_like(fresh)
    for u in range(STEPS):
        for kind in range(2):
            fresh[kind, u : u + 1, :] = new_ref[u, r_own, kind : kind + 1, :].astype(F32)
    queries = jnp.concatenate([block_diagonal(rows, me, g) for g in range(3)], axis=0).astype(BF16)
    live = iota((24, 16), 1) <= t_own
    out, lse = softmax_parts(queries, fresh[0].astype(BF16), fresh[1].astype(BF16), live)
    ((fresh_first, fresh_second),) = message_tiles(out, lse, 3)

    for load in page_loads:
        load.wait()

    def attend(r):
        both = jnp.concatenate(
            [
                jnp.concatenate([pages[c, table_ref[r, j]].reshape(128, 128) for j in range(8)], axis=0)
                for c in range(4)
            ],
            axis=1,
        )
        queries = jnp.concatenate(
            [block_diagonal(rows, REQS * t + r, g) for t in range(STEPS) for g in range(3)], axis=0
        ).astype(BF16)
        lane = iota((96, 1024), 1)
        live = (lane // 2 + me * 512 < len_ref[r]) & (lane % 2 == 0)
        out, lse = softmax_parts(queries, both, None, live)
        for t, (first, second) in enumerate(message_tiles(out, lse, 12)):
            msg[REQS * t + r, 0:8, :] = first
            msg[REQS * t + r, 8:16, :] = second

    def attend_some(step, c):
        for i in range(TOGETHER):
            attend(step * TOGETHER + i)

        @pl.when(step == 0)
        def _():
            pl.semaphore_wait(barrier, N_SEQ + N_EXP - 2)
            lax.fori_loop(1, N_EXP, send_mask, 0)
            lax.fori_loop(1, N_X, send_weights, 0)

        for i in range(TOGETHER):
            for t in range(STEPS):
                d = REQS * t + step * TOGETHER + i

                @pl.when(d != me)
                def _():
                    push(msg.at[d], recv1.at[me], 0, seq=d)

        return c

    lax.fori_loop(0, REQS // TOGETHER, attend_some, 0)
    recv1[me] = msg[me]

    loads[8].wait()
    low = iota((SLICE, 128), 1) < 64

    def wo_tile(i):
        return wo_ref[:, 128 * i : 128 * i + 128].astype(F32)

    tiles = []
    for k in range(8):
        if k % 2 == 0:
            tiles.append(wo_tile(3 * k // 2))
        else:
            tiles.append(jnp.where(low, wo_tile((3 * k + 1) // 2), wo_tile((3 * k - 1) // 2)))
    for k in range(8):
        tiles.append(wo_tile((3 * k + 2) // 2))
    wo = jnp.concatenate(tiles, axis=1).astype(BF16)

    def join(ref):
        halves = []
        for h in range(2):
            joined = ref[4 * h].astype(F32)
            for i in range(1, 4):
                part = pltpu.roll(ref[4 * h + i].astype(F32), 32 * i, 1)
                joined = jnp.where(lane48 // 32 == i, part, joined)
            halves.append(joined)
        return jnp.concatenate(halves, axis=1)

    drain(recv_sems, 1, mbuf.at[pl.ds(0, N_EXP - 1)])
    mask = join(mbuf)
    row, col = iota((ALL_TOKENS, ALL_TOKENS), 0), iota((ALL_TOKENS, ALL_TOKENS), 1)
    earlier = jnp.where((row // 8 == col // 8) & (row < col), 1.0, 0.0).astype(BF16)
    rank = nn_dot(mask.astype(BF16), earlier)
    group = (iota((SLICE, ALL_TOKENS), 1) // 8 * 4).astype(F32)
    slot[...] = jnp.where(mask > 0.5, group + rank, -1.0)
    slot_row = iota((SLOTS, ALL_TOKENS), 0).astype(F32)
    for j in range(EXPERTS_LOCAL):
        slots = slot[pl.ds(ex * EXPERTS_LOCAL + j, 1), :]
        hot = jnp.where(slot_row == slots, 1.0, 0.0).astype(BF16)
        spread[j] = hot
        spread_t[j] = hot.T
    mask_one = mbuf[z_own]
    row, col = iota((128, 128), 0), iota((128, 128), 1)
    earlier = jnp.where((row // 8 == col // 8) & (row < col), 1.0, 0.0).astype(BF16)
    rank = nn_dot(mask_one, earlier)
    group = (lane48 // 8 * 4).astype(F32)
    slot_z[...] = jnp.where((mask_one.astype(F32) > 0.5) & (lane48 < TOKENS), group + rank, -1.0)
    slot_row = iota((OWN_SLOTS, 128), 0).astype(F32)
    for j in range(EXPERTS_LOCAL):
        slots = slot_z[pl.ds(ex * EXPERTS_LOCAL + j, 1), :]
        gather_z[OWN_SLOTS * j : OWN_SLOTS * j + OWN_SLOTS, :] = jnp.where(slot_row == slots, 1.0, 0.0).astype(BF16)
    flip[...] = jnp.zeros_like(flip)
    flip[0:SLICE, :] = mask_one.astype(F32)
    mask_z[...] = flip[...].T[0:TOKENS]

    drain(recv_sems, 0, recv1.at[pl.ds(0, N_SEQ - 1)])
    head = iota((8, 128), 0)
    lane = iota((8, 128), 1)
    odd = head % 2 == 1
    half = lane // 64 == head % 2

    def stat_of(second):
        return jnp.where(odd, second, pltpu.roll(second, 64, 1))

    largest = lax.fori_loop(
        0, N_SEQ, lambda s, m: jnp.maximum(m, stat_of(recv1[s, 8:16, :])), stat_of(fresh_second), unroll=8
    )

    def add_part(first, second, carry):
        total, acc1, acc2 = carry
        w = jnp.exp(stat_of(second) - largest)
        w1 = jnp.where(half, w[:, 0:1], w[:, 1:2])
        return total + w, acc1 + w1 * first, acc2 + w[:, 2:3] * second

    zero = jnp.zeros((8, 128), F32)
    carry = add_part(fresh_first, fresh_second, (zero, zero, zero))
    total, acc1, acc2 = lax.fori_loop(
        0, N_SEQ, lambda s, c: add_part(recv1[s, 0:8, :], recv1[s, 8:16, :], c), carry, unroll=8
    )
    att1 = acc1 / jnp.where(half, total[:, 0:1], total[:, 1:2])
    att2 = jnp.where(half, acc2 / total[:, 2:3], 0.0)
    token = jnp.concatenate([att1, att2], axis=0).astype(BF16)
    send2[...] = token
    recv2[me] = token

    def send_token(i, c):
        push(send2, recv2.at[me], 3, seq=seq_peer(i))
        return c

    lax.fori_loop(1, N_SEQ, send_token, 0)

    drain(recv_sems, 3, recv2.at[pl.ds(0, N_SEQ - 1)])
    attf[...] = recv2[...].astype(F32).reshape(N_SEQ * 16, 128)
    att = jnp.concatenate([attf[pl.ds(j, N_SEQ, stride=16), :] for j in range(16)], axis=1).astype(BF16)
    hidden = residual + nt_dot(wo, att)
    hid[...] = hidden
    xstage[...] = jnp.zeros_like(xstage)
    xstage[:, 0:TOKENS] = (hidden * gain).astype(BF16)
    xbuf[ex] = xstage[...]

    def send_x(i, c):
        push(xstage, xbuf.at[ex], 4, exp=exp_peer(i))
        return c

    lax.fori_loop(1, N_EXP, send_x, 0)

    drain(recv_sems, 4, xbuf.at[pl.ds(0, N_EXP - 1)])
    x4[...] = join(xbuf).astype(BF16)
    xq[x_own] = x4[...]

    def send_plane(i, c):
        push(x4, xq.at[x_own], 5, seq=x_peer(i) * N_Z + z_own)
        return c

    lax.fori_loop(1, N_X, send_plane, 0)

    drain(recv_sems, 2, wbuf.at[pl.ds(0, N_X - 1)])
    drain(recv_sems, 10, rbuf.at[pl.ds(0, N_X - 1)])
    for j in range(EXPERTS_LOCAL):
        down[:, 128 * j : 128 * j + 128] = wbuf[:, j, :, 256:384].reshape(PLANE, 128)
    drain(recv_sems, 5, xq.at[pl.ds(0, N_X - 1)])
    x_plane = xq[...].reshape(PLANE, ALL_TOKENS)
    for j in range(EXPERTS_LOCAL):
        x_slots = nt_dot(spread[j], x_plane).astype(BF16)
        pre = nn_dot(x_slots, wbuf[:, j, :, 0:256].reshape(PLANE, 256)).astype(BF16)
        at = OWN_SLOTS * j
        pstage[:, at : at + OWN_SLOTS, :] = pre[:, 0:128].reshape(N_Z, OWN_SLOTS, 128)
        at += LOCAL_SLOTS
        pstage[:, at : at + OWN_SLOTS, :] = pre[:, 128:256].reshape(N_Z, OWN_SLOTS, 128)
    same = iota((ALL_TOKENS, ALL_TOKENS), 0) == iota((ALL_TOKENS, ALL_TOKENS), 1)
    x_tokens = nt_dot(jnp.where(same, 1.0, 0.0).astype(BF16), x_plane)
    routing = rbuf[...].reshape(PLANE, 128)
    stats = jnp.where(
        iota((ALL_TOKENS, 128), 1) < EXPERTS,
        nn_dot(x_tokens.astype(BF16), routing),
        nn_dot((x_tokens * x_tokens).astype(BF16), routing),
    )
    stats = jnp.where(iota((ALL_TOKENS, 128), 1) < 42, stats, 0.0)
    stats_high = stats.astype(BF16).astype(F32)
    stats = stats_high + pltpu.roll(stats - stats_high, 64, 1)
    pstage[:, 2 * LOCAL_SLOTS :, :] = stats.astype(BF16).reshape(N_Z, TOKENS, 128)
    pbuf[z_own] = pstage[z_own]

    def send_partial(i, c):
        z = z_peer(i)
        push(pstage.at[z], pbuf.at[z_own], 6, seq=x_own * N_Z + z)
        return c

    lax.fori_loop(1, N_Z, send_partial, 0)
    drain(recv_sems, 6, pbuf.at[pl.ds(0, N_Z - 1)])
    whole = pbuf[0].astype(F32)
    for i in range(1, N_Z):
        whole = whole + pbuf[i].astype(F32)
    stats = whole[2 * LOCAL_SLOTS :]
    stats = stats + pltpu.roll(stats, 64, 1)
    inv_rms = lax.rsqrt((stats[:, 40:41] + stats[:, 41:42]) / D + 1e-6)
    powers = jnp.where(mask_z[...] > 0.5, jnp.exp(stats * inv_rms), 0.0)
    gates = powers / jnp.sum(powers, axis=1, keepdims=True)
    gates = jnp.where(iota((TOKENS, 128), 1) == 64, inv_rms, gates)
    gates = jnp.concatenate([gates, jnp.zeros((128 - TOKENS, 128), F32)], axis=0)
    gates_high = gates.astype(BF16)
    gates_low = (gates - gates_high.astype(F32)).astype(BF16)
    per_slot = nn_dot(gather_z[...], gates_high) + nn_dot(gather_z[...], gates_low)
    row, col = iota((LOCAL_SLOTS, 128), 0), iota((LOCAL_SLOTS, 128), 1)
    own_gate = jnp.where(col == ex * EXPERTS_LOCAL + row // OWN_SLOTS, per_slot, 0.0)
    gate_weight = jnp.sum(own_gate, axis=1, keepdims=True)
    slot_rms = per_slot[:, 64:65]
    gate = whole[0:LOCAL_SLOTS] * slot_rms
    up = whole[LOCAL_SLOTS : 2 * LOCAL_SLOTS] * slot_rms
    istage[...] = (gate / (1.0 + jnp.exp(-gate)) * up * gate_weight).astype(BF16)
    ibuf[z_own] = istage[...]

    def send_inner(i, c):
        push(istage, ibuf.at[z_own], 7, seq=x_own * N_Z + z_peer(i))
        return c

    lax.fori_loop(1, N_Z, send_inner, 0)
    drain(recv_sems, 7, ibuf.at[pl.ds(0, N_Z - 1)])
    inner = []
    for j in range(EXPERTS_LOCAL):
        at = OWN_SLOTS * j
        slots = ibuf[:, at : at + OWN_SLOTS, :].reshape(SLOTS, 128)
        inner.append(nn_dot(spread_t[j], slots).astype(BF16))
    ystage[...] = nt_dot(down[...], jnp.concatenate(inner, axis=1)).astype(BF16).reshape(N_X, SLICE, ALL_TOKENS)
    ybuf[x_own] = ystage[x_own]

    def send_y(i, c):
        x = x_peer(i)
        push(ystage.at[x], ybuf.at[x_own], 8, seq=x * N_Z + z_own)
        return c

    lax.fori_loop(1, N_X, send_y, 0)
    drain(recv_sems, 8, ybuf.at[pl.ds(0, N_X - 1)])
    summed = ybuf[0].astype(F32)
    for i in range(1, N_X):
        summed = summed + ybuf[i].astype(F32)
    for e in range(N_EXP):
        part = summed[:, 128 * (e // 4) : 128 * (e // 4) + 128]
        if e % 4:
            part = pltpu.roll(part, 128 - 32 * (e % 4), 1)
        zstage[e] = part.astype(BF16)
    zbuf[ex] = zstage[ex]

    def send_z(i, c):
        e = exp_peer(i)
        push(zstage.at[e], zbuf.at[ex], 9, exp=e)
        return c

    lax.fori_loop(1, N_EXP, send_z, 0)
    drain(recv_sems, 9, zbuf.at[pl.ds(0, N_EXP - 1)])
    moe = jnp.sum(zbuf[...].astype(F32), axis=0)
    flip[0:SLICE, :] = moe
    flip[0:SLICE, 0:TOKENS] = moe[:, 0:TOKENS] + hid[...]
    out = flip[...].T
    out_ref[...] = out[0:TOKENS, 0:SLICE].reshape(STEPS, REQS, SLICE).astype(BF16)

    drain(send_sems, 0, recv1.at[pl.ds(0, N_SEQ - 1)])
    drain(send_sems, 1, mbuf.at[pl.ds(0, N_EXP - 1)])
    drain(send_sems, 3, recv2.at[pl.ds(0, N_SEQ - 1)])
    drain(send_sems, 4, xbuf.at[pl.ds(0, N_EXP - 1)])
    drain(send_sems, 2, wbuf.at[pl.ds(0, N_X - 1)])
    drain(send_sems, 10, rbuf.at[pl.ds(0, N_X - 1)])
    drain(send_sems, 5, xq.at[pl.ds(0, N_X - 1)])
    drain(send_sems, 6, pbuf.at[pl.ds(0, N_Z - 1)])
    drain(send_sems, 7, ibuf.at[pl.ds(0, N_Z - 1)])
    drain(send_sems, 8, ybuf.at[pl.ds(0, N_X - 1)])
    drain(send_sems, 9, zbuf.at[pl.ds(0, N_EXP - 1)])


def layer(page_table, cache_len, *arrays):
    smem = pl.BlockSpec(memory_space=pltpu.SMEM)
    hbm = pl.BlockSpec(memory_space=pltpu.HBM)
    return pl.pallas_call(
        layer_kernel,
        out_shape=jax.ShapeDtypeStruct((STEPS, REQS, SLICE), BF16),
        in_specs=[smem, smem] + [hbm] * 10,
        out_specs=pl.BlockSpec(memory_space=pltpu.VMEM),
        scratch_shapes=[
            VMEM((STEPS, REQS, D), BF16),
            VMEM((STEPS, REQS, 2, 512), BF16),
            VMEM((4, 64, 64, 2, 128), BF16),
            VMEM((SLICE, D), BF16),
            VMEM((STEPS, REQS, SLICE), BF16),
            VMEM((1, SLICE), F32),
            VMEM((EXPERTS, SLICE), BF16),
            VMEM((EXPERTS_LOCAL, SLICE, 2, 512), BF16),
            VMEM((EXPERTS_LOCAL, SLICE, 512), BF16),
            VMEM((STEPS, REQS, 8), jnp.int32),
            VMEM((TOKENS, D), F32),
            VMEM((2, 16, 512), F32),
            VMEM((N_SEQ, 16, 128), F32),
            VMEM((128, 128), F32),
            VMEM((N_SEQ, 16, 128), F32),
            VMEM((16, 128), BF16),
            VMEM((N_SEQ, 16, 128), BF16),
            VMEM((N_SEQ * 16, 128), F32),
            VMEM((N_X, EXPERTS_LOCAL, SLICE, 384), BF16),
            VMEM((N_X, EXPERTS_LOCAL, SLICE, 384), BF16),
            VMEM((N_X, SLICE, 128), BF16),
            VMEM((SLICE, 128), BF16),
            VMEM((N_EXP, SLICE, 128), BF16),
            VMEM((SLICE, 128), BF16),
            VMEM((N_EXP, SLICE, 128), BF16),
            VMEM((SLICE, ALL_TOKENS), F32),
            VMEM((SLICE, 128), F32),
            VMEM((EXPERTS_LOCAL, SLOTS, ALL_TOKENS), BF16),
            VMEM((EXPERTS_LOCAL, ALL_TOKENS, SLOTS), BF16),
            VMEM((LOCAL_SLOTS, 128), BF16),
            VMEM((TOKENS, 128), F32),
            VMEM((PLANE, 128 * EXPERTS_LOCAL), BF16),
            VMEM((SLICE, ALL_TOKENS), BF16),
            VMEM((N_X, SLICE, ALL_TOKENS), BF16),
            VMEM((N_Z, 2 * LOCAL_SLOTS + TOKENS, 128), BF16),
            VMEM((N_Z, 2 * LOCAL_SLOTS + TOKENS, 128), BF16),
            VMEM((LOCAL_SLOTS, 128), BF16),
            VMEM((N_Z, LOCAL_SLOTS, 128), BF16),
            VMEM((N_X, SLICE, ALL_TOKENS), BF16),
            VMEM((N_X, SLICE, ALL_TOKENS), BF16),
            VMEM((N_EXP, SLICE, 128), BF16),
            VMEM((N_EXP, SLICE, 128), BF16),
            VMEM((SLICE, TOKENS), F32),
            pltpu.SemaphoreType.DMA((9,)),
            pltpu.SemaphoreType.DMA((32,)),
            pltpu.SemaphoreType.DMA((11,)),
            pltpu.SemaphoreType.DMA((11,)),
        ],
        compiler_params=pltpu.CompilerParams(
            collective_id=0, has_side_effects=True, vmem_limit_bytes=60 << 20
        ),
        name="layer",
    )(page_table, cache_len, *arrays)


def local(
    queries,
    new_key_value,
    key_value_cache,
    page_table,
    cache_len,
    routes,
    residual,
    w_out,
    norm_gain,
    w_router,
    w_gate_up,
    w_down,
):
    cache = key_value_cache.reshape(64, 64, 2, 4, 128).transpose(0, 1, 3, 2, 4)
    return layer(
        page_table, cache_len, queries, new_key_value, cache, w_out.T, residual, norm_gain.reshape(1, SLICE),
        w_router.T, w_gate_up, w_down, routes,
    )


def solution(mesh):
    in_specs = (
        P(None, "exp", None),
        P(None, "exp", None, None),
        P("exp", "seq", None, None, None),
        P("exp", "seq"),
        P("exp"),
        P(None, "exp", None),
        P(None, "exp", "seq"),
        P(None, "seq"),
        P("seq"),
        P("seq", None),
        P("exp", "seq", None, None),
        P("exp", "seq", None),
    )
    out_specs = P(None, "exp", "seq")
    return jax.shard_map(local, mesh=mesh, in_specs=in_specs, out_specs=out_specs, check_vma=False)
```

```python
import jax
import jax.numpy as jnp
from jax import lax
from jax.experimental import pallas as pl
from jax.experimental.pallas import tpu as pltpu
from jax.sharding import PartitionSpec as P

NEG = -1e30
N_SEQ = 32
N_EXP = 8
STEPS = 4
REQS = 8
TOKENS = STEPS * REQS
EXPERTS = 40
EXPERTS_LOCAL = 5
OWN_SLOTS = 16
LOCAL_SLOTS = EXPERTS_LOCAL * OWN_SLOTS
TOGETHER = 2
SLOTS = 128
SLICE = 48
N_X = 4
N_Z = 8
PLANE = N_X * SLICE
N_PLANE = N_X * N_EXP
D = 1536
ALL_TOKENS = TOKENS * N_EXP
F32 = jnp.float32
BF16 = jnp.bfloat16
MESH = pl.DeviceIdType.MESH
VMEM = pltpu.VMEM


def iota(shape, axis):
    return lax.broadcasted_iota(jnp.int32, shape, axis)


def nt_dot(a, b):
    return lax.dot_general(a, b, (((1,), (1,)), ((), ())), preferred_element_type=F32)


def nn_dot(a, b):
    return lax.dot_general(a, b, (((1,), (0,)), ((), ())), preferred_element_type=F32)


def spread_queries(q_ref, rows_ref):
    low = iota((REQS, 128), 1) < 64
    for t in range(STEPS):
        q = q_ref[t].astype(F32) * 0.125
        tiles = [q[:, 128 * i : 128 * i + 128] for i in range(12)]
        for g in range(3):
            for pair in range(4):
                first, second = 6 * pair + g, 6 * pair + 3 + g
                if g == 1:
                    tile = jnp.where(low, tiles[second // 2], tiles[first // 2])
                    tile = pltpu.roll(tile, 64, 1)
                else:
                    tile = jnp.where(low, tiles[first // 2], tiles[second // 2])
                base = g * 512 + pair * 128
                rows_ref[REQS * t : REQS * t + REQS, base : base + 128] = tile


def block_diagonal(rows_ref, row, g):
    own = iota((8, 512), 1) // 64 == iota((8, 512), 0)
    values = rows_ref[pl.ds(row, 1), 512 * g : 512 * g + 512]
    return jnp.where(own, jnp.broadcast_to(values, (8, 512)), 0.0)


def softmax_parts(queries, keys, values, live):
    scores = jnp.where(live, nt_dot(queries, keys), NEG)
    largest = jnp.max(scores, axis=1, keepdims=True)
    weights = jnp.where(live, jnp.exp(scores - largest), 0.0)
    total = jnp.sum(weights, axis=1, keepdims=True)
    if values is None:
        acc = nn_dot(pltpu.roll(weights, 1, 1).astype(BF16), keys)
    else:
        acc = nn_dot(weights.astype(BF16), values)
    some = total > 0.0
    safe = jnp.where(some, total, 1.0)
    return acc / safe, jnp.where(some, largest + jnp.log(safe), NEG)


def message_tiles(out, lse, groups):
    out = out.reshape(groups, 8, 512)
    lse = lse.reshape(groups, 8, 1)
    head = iota((groups, 8, 128), 1)
    lane = iota((groups, 8, 128), 2)
    packed = out[:, :, 0:128]
    for j in range(1, 4):
        packed = jnp.where(head // 2 == j, out[:, :, 128 * j : 128 * j + 128], packed)
    packed = jnp.where(lane // 64 == head % 2, packed, 0.0)
    head, lane = head[0], lane[0]
    free = lane // 64 != head % 2
    place = lane % 64
    tiles = []
    for t in range(groups // 3):
        first = packed[3 * t] + pltpu.roll(packed[3 * t + 1], 64, 1)
        stat = jnp.where(place == 0, lse[3 * t], jnp.where(place == 1, lse[3 * t + 1], lse[3 * t + 2]))
        second = packed[3 * t + 2] + jnp.where(free & (place < 3), stat, 0.0)
        tiles.append((first, second))
    return tiles


def layer_kernel(
    table_ref, len_ref, q_hbm, new_hbm, kv_hbm, wo_hbm, res_hbm, gain_hbm, wr_hbm, wgu_hbm, wd_hbm, routes_hbm,
    out_ref,
    q_ref, new_ref, pages, wo_ref, res_ref, gain_ref, wr_ref, wgu_ref, wd_ref, routes_ref,
    rows, fresh, msg, flip, recv1, send2, recv2, attf, wstage, wbuf, rbuf, mstage, mbuf, xstage, xbuf,
    slot, slot_z, spread, spread_t, gather_z, mask_z, down, xq, pstage, pbuf, istage, ibuf,
    zstage, zbuf, hid, in_sems, page_sems, send_sems, recv_sems,
):
    me = lax.axis_index("seq")
    ex = lax.axis_index("exp")
    x_own, z_own = lax.div(me, N_Z), lax.rem(me, N_Z)

    def seq_peer(i):
        return lax.rem(me + i, N_SEQ)

    def exp_peer(i):
        return lax.rem(ex + i, N_EXP)

    def x_peer(i):
        return lax.rem(x_own + i, N_X)

    def plane_peer(i):
        place = lax.rem(x_own * N_EXP + ex + i, N_PLANE)
        return lax.div(place, N_EXP), lax.rem(place, N_EXP)

    def z_peer(i):
        return lax.rem(z_own + i, N_Z)

    def push(src, dst, phase, seq=None, exp=None):
        target = (me if seq is None else seq, ex if exp is None else exp)
        pltpu.make_async_remote_copy(
            src_ref=src, dst_ref=dst, send_sem=send_sems.at[phase], recv_sem=recv_sems.at[phase],
            device_id=target, device_id_type=MESH,
        ).start()

    def drain(sems, phase, ref):
        pltpu.make_async_copy(ref, ref, sems.at[phase]).wait()

    loads = [
        pltpu.make_async_copy(src, dst, in_sems.at[i])
        for i, (src, dst) in enumerate(
            (
                (wgu_hbm, wgu_ref), (wd_hbm, wd_ref), (res_hbm, res_ref), (gain_hbm, gain_ref), (wr_hbm, wr_ref),
                (routes_hbm, routes_ref), (q_hbm, q_ref), (new_hbm, new_ref), (wo_hbm, wo_ref),
            )
        )
    ]
    for load in loads:
        load.start()
    page_loads = [
        pltpu.make_async_copy(
            kv_hbm.at[8 * i : 8 * i + 8, :, c], pages.at[c, 8 * i : 8 * i + 8], page_sems.at[4 * i + c]
        )
        for i in range(8)
        for c in range(4)
    ]
    for load in page_loads:
        load.start()

    lane16 = iota((16, 128), 1)

    def turn(tile, quarters):
        return pltpu.roll(tile, 32 * (quarters % 4), 1) if quarters % 4 else tile

    def pack(groups, quarter):
        packed = turn(groups[2], 2 - quarter)
        for b in range(2):
            packed = jnp.where(lane16 // 32 == b, turn(groups[b], b - quarter), packed)
        return packed

    def drain_plane(sems, phase):
        drain(sems, phase, recv2.at[pl.ds(0, N_PLANE - 1)])

    barrier = pltpu.get_barrier_semaphore()

    def greet_seq(i, c):
        pl.semaphore_signal(barrier, inc=1, device_id=(seq_peer(i), ex), device_id_type=MESH)
        return c

    def greet_plane(i, c):
        x, e = plane_peer(i)
        pl.semaphore_signal(barrier, inc=1, device_id=(x * N_Z + z_own, e), device_id_type=MESH)
        return c

    lax.fori_loop(1, N_SEQ, greet_seq, 0)
    lax.fori_loop(1, N_PLANE, greet_plane, 0)

    for load in loads[:6]:
        load.wait()
    flip[...] = jnp.zeros_like(flip)
    flip[0:TOKENS, 0:SLICE] = res_ref[...].reshape(TOKENS, SLICE).astype(F32)
    flip[TOKENS : TOKENS + 1, 0:SLICE] = gain_ref[...]
    flip[40:80, 0:SLICE] = wr_ref[...].astype(F32)
    flip[0:TOKENS, 64:72] = routes_ref[...].reshape(TOKENS, 8).astype(F32)
    turned = flip[...].T
    top = turned[0:SLICE]
    lane48 = iota((SLICE, 128), 1)
    residual = top[:, 0:TOKENS]
    gain = top[:, TOKENS : TOKENS + 1]
    inv_gain = 1.0 / (gain * gain)
    inv_high = inv_gain.astype(BF16).astype(F32)
    router = pltpu.roll(top, 88, 1)
    router = jnp.where(lane48 == 40, inv_high, jnp.where(lane48 == 41, inv_gain - inv_high, router))
    router = jnp.where(lane48 < 42, router, 0.0).astype(BF16)
    expert_row = iota((SLICE, 128), 0).astype(F32)
    chosen = jnp.zeros((SLICE, 128), F32)
    for k in range(8):
        chosen = jnp.where(expert_row == turned[64 + k : 65 + k, :], 1.0, chosen)
    mstage[...] = chosen.astype(BF16)
    mbuf[ex] = chosen.astype(BF16)

    for j in range(EXPERTS_LOCAL):
        for c in range(N_X):
            cols = slice(128 * c, 128 * c + 128)
            wstage[c, j, :, 0:128] = wgu_ref[j, :, 0, cols]
            wstage[c, j, :, 128:256] = wgu_ref[j, :, 1, cols]
            wstage[c, j, :, 256:384] = wd_ref[j, :, cols]
    wbuf[x_own] = wstage[x_own]
    rbuf[x_own] = router

    def send_mask(i, c):
        push(mstage, mbuf.at[ex], 1, exp=exp_peer(i))
        return c

    def send_weights(i, c):
        x = x_peer(i)
        push(wstage.at[x], wbuf.at[x_own], 2, seq=x * N_Z + z_own)
        push(rbuf.at[x_own], rbuf.at[x_own], 10, seq=x * N_Z + z_own)
        return c

    for load in loads[6:8]:
        load.wait()
    spread_queries(q_ref, rows)
    t_own, r_own = lax.div(me, 8), lax.rem(me, 8)
    fresh[...] = jnp.zeros_like(fresh)
    for u in range(STEPS):
        for kind in range(2):
            fresh[kind, u : u + 1, :] = new_ref[u, r_own, kind : kind + 1, :].astype(F32)
    queries = jnp.concatenate([block_diagonal(rows, me, g) for g in range(3)], axis=0).astype(BF16)
    live = iota((24, 16), 1) <= t_own
    out, lse = softmax_parts(queries, fresh[0].astype(BF16), fresh[1].astype(BF16), live)
    ((fresh_first, fresh_second),) = message_tiles(out, lse, 3)

    for load in page_loads:
        load.wait()

    def attend(r):
        both = jnp.concatenate(
            [
                jnp.concatenate([pages[c, table_ref[r, j]].reshape(128, 128) for j in range(8)], axis=0)
                for c in range(4)
            ],
            axis=1,
        )
        queries = jnp.concatenate(
            [block_diagonal(rows, REQS * t + r, g) for t in range(STEPS) for g in range(3)], axis=0
        ).astype(BF16)
        lane = iota((96, 1024), 1)
        live = (lane // 2 + me * 512 < len_ref[r]) & (lane % 2 == 0)
        out, lse = softmax_parts(queries, both, None, live)
        for t, (first, second) in enumerate(message_tiles(out, lse, 12)):
            msg[REQS * t + r, 0:8, :] = first
            msg[REQS * t + r, 8:16, :] = second

    def attend_some(step, c):
        for i in range(TOGETHER):
            attend(step * TOGETHER + i)

        @pl.when(step == 0)
        def _():
            pl.semaphore_wait(barrier, N_SEQ + N_PLANE - 2)
            lax.fori_loop(1, N_EXP, send_mask, 0)
            lax.fori_loop(1, N_X, send_weights, 0)

        for i in range(TOGETHER):
            for t in range(STEPS):
                d = REQS * t + step * TOGETHER + i

                @pl.when(d != me)
                def _():
                    push(msg.at[d], recv1.at[me], 0, seq=d)

        return c

    lax.fori_loop(0, REQS // TOGETHER, attend_some, 0)
    recv1[me] = msg[me]

    loads[8].wait()
    low = iota((SLICE, 128), 1) < 64

    def wo_tile(i):
        return wo_ref[:, 128 * i : 128 * i + 128].astype(F32)

    tiles = []
    for k in range(8):
        if k % 2 == 0:
            tiles.append(wo_tile(3 * k // 2))
        else:
            tiles.append(jnp.where(low, wo_tile((3 * k + 1) // 2), wo_tile((3 * k - 1) // 2)))
    for k in range(8):
        tiles.append(wo_tile((3 * k + 2) // 2))
    wo = jnp.concatenate(tiles, axis=1).astype(BF16)

    def join(ref):
        halves = []
        for h in range(2):
            joined = ref[4 * h].astype(F32)
            for i in range(1, 4):
                part = pltpu.roll(ref[4 * h + i].astype(F32), 32 * i, 1)
                joined = jnp.where(lane48 // 32 == i, part, joined)
            halves.append(joined)
        return jnp.concatenate(halves, axis=1)

    drain(recv_sems, 1, mbuf.at[pl.ds(0, N_EXP - 1)])
    mask = join(mbuf)
    row, col = iota((ALL_TOKENS, ALL_TOKENS), 0), iota((ALL_TOKENS, ALL_TOKENS), 1)
    earlier = jnp.where((row // 8 == col // 8) & (row < col), 1.0, 0.0).astype(BF16)
    rank = nn_dot(mask.astype(BF16), earlier)
    group = (iota((SLICE, ALL_TOKENS), 1) // 8 * 4).astype(F32)
    slot[...] = jnp.where(mask > 0.5, group + rank, -1.0)
    slot_row = iota((SLOTS, ALL_TOKENS), 0).astype(F32)
    for j in range(EXPERTS_LOCAL):
        slots = slot[pl.ds(ex * EXPERTS_LOCAL + j, 1), :]
        hot = jnp.where(slot_row == slots, 1.0, 0.0).astype(BF16)
        spread[j] = hot
        spread_t[j] = hot.T
    mask_one = mbuf[z_own]
    row, col = iota((128, 128), 0), iota((128, 128), 1)
    earlier = jnp.where((row // 8 == col // 8) & (row < col), 1.0, 0.0).astype(BF16)
    rank = nn_dot(mask_one, earlier)
    group = (lane48 // 8 * 4).astype(F32)
    slot_z[...] = jnp.where((mask_one.astype(F32) > 0.5) & (lane48 < TOKENS), group + rank, -1.0)
    slot_row = iota((OWN_SLOTS, 128), 0).astype(F32)
    for j in range(EXPERTS_LOCAL):
        slots = slot_z[pl.ds(ex * EXPERTS_LOCAL + j, 1), :]
        gather_z[OWN_SLOTS * j : OWN_SLOTS * j + OWN_SLOTS, :] = jnp.where(slot_row == slots, 1.0, 0.0).astype(BF16)
    flip[...] = jnp.zeros_like(flip)
    flip[0:SLICE, :] = mask_one.astype(F32)
    mask_z[...] = flip[...].T[0:TOKENS]

    drain(recv_sems, 0, recv1.at[pl.ds(0, N_SEQ - 1)])
    head = iota((8, 128), 0)
    lane = iota((8, 128), 1)
    odd = head % 2 == 1
    half = lane // 64 == head % 2

    def stat_of(second):
        return jnp.where(odd, second, pltpu.roll(second, 64, 1))

    largest = lax.fori_loop(
        0, N_SEQ, lambda s, m: jnp.maximum(m, stat_of(recv1[s, 8:16, :])), stat_of(fresh_second), unroll=8
    )

    def add_part(first, second, carry):
        total, acc1, acc2 = carry
        w = jnp.exp(stat_of(second) - largest)
        w1 = jnp.where(half, w[:, 0:1], w[:, 1:2])
        return total + w, acc1 + w1 * first, acc2 + w[:, 2:3] * second

    zero = jnp.zeros((8, 128), F32)
    carry = add_part(fresh_first, fresh_second, (zero, zero, zero))
    total, acc1, acc2 = lax.fori_loop(
        0, N_SEQ, lambda s, c: add_part(recv1[s, 0:8, :], recv1[s, 8:16, :], c), carry, unroll=8
    )
    att1 = acc1 / jnp.where(half, total[:, 0:1], total[:, 1:2])
    att2 = jnp.where(half, acc2 / total[:, 2:3], 0.0)
    token = jnp.concatenate([att1, att2], axis=0).astype(BF16)
    send2[...] = token
    recv2[me] = token

    def send_token(i, c):
        push(send2, recv2.at[me], 3, seq=seq_peer(i))
        return c

    lax.fori_loop(1, N_SEQ, send_token, 0)

    drain(recv_sems, 3, recv2.at[pl.ds(0, N_SEQ - 1)])
    attf[...] = recv2[...].astype(F32).reshape(N_SEQ * 16, 128)
    att = jnp.concatenate([attf[pl.ds(j, N_SEQ, stride=16), :] for j in range(16)], axis=1).astype(BF16)
    hidden = residual + nt_dot(wo, att)
    hid[...] = hidden
    flip[0:SLICE, 0:TOKENS] = hidden * gain
    scaled = flip[0:SLICE, :]
    xstage[...] = pack([scaled[16 * b : 16 * b + 16] for b in range(3)], 0).astype(BF16)
    xbuf[x_own, ex] = xstage[...]

    def send_x(i, c):
        x, e = plane_peer(i)
        push(xstage, xbuf.at[x_own, ex], 4, seq=x * N_Z + z_own, exp=e)
        return c

    lax.fori_loop(1, N_PLANE, send_x, 0)

    drain(recv_sems, 2, wbuf.at[pl.ds(0, N_X - 1)])
    drain(recv_sems, 10, rbuf.at[pl.ds(0, N_X - 1)])
    for j in range(EXPERTS_LOCAL):
        down[:, 128 * j : 128 * j + 128] = wbuf[:, j, :, 256:384].reshape(PLANE, 128)
    drain_plane(recv_sems, 4)
    for x in range(N_X):
        for h in range(2):
            blocks = [xbuf[x, 4 * h + i].astype(F32) for i in range(4)]
            for b in range(3):
                joined = turn(blocks[0], -b)
                for i in range(1, 4):
                    joined = jnp.where(lane16 // 32 == i, turn(blocks[i], i - b), joined)
                xq[x, 16 * b : 16 * b + 16, 128 * h : 128 * h + 128] = joined.astype(BF16)
    x_plane = xq[...].reshape(PLANE, ALL_TOKENS)
    for j in range(EXPERTS_LOCAL):
        x_slots = nt_dot(spread[j], x_plane).astype(BF16)
        pre = nn_dot(x_slots, wbuf[:, j, :, 0:256].reshape(PLANE, 256)).astype(BF16)
        at = OWN_SLOTS * j
        pstage[:, at : at + OWN_SLOTS, :] = pre[:, 0:128].reshape(N_Z, OWN_SLOTS, 128)
        at += LOCAL_SLOTS
        pstage[:, at : at + OWN_SLOTS, :] = pre[:, 128:256].reshape(N_Z, OWN_SLOTS, 128)
    same = iota((ALL_TOKENS, ALL_TOKENS), 0) == iota((ALL_TOKENS, ALL_TOKENS), 1)
    x_tokens = nt_dot(jnp.where(same, 1.0, 0.0).astype(BF16), x_plane)
    routing = rbuf[...].reshape(PLANE, 128)
    stats = jnp.where(
        iota((ALL_TOKENS, 128), 1) < EXPERTS,
        nn_dot(x_tokens.astype(BF16), routing),
        nn_dot((x_tokens * x_tokens).astype(BF16), routing),
    )
    stats = jnp.where(iota((ALL_TOKENS, 128), 1) < 42, stats, 0.0)
    stats_high = stats.astype(BF16).astype(F32)
    stats = stats_high + pltpu.roll(stats - stats_high, 64, 1)
    pstage[:, 2 * LOCAL_SLOTS :, :] = stats.astype(BF16).reshape(N_Z, TOKENS, 128)
    pbuf[z_own] = pstage[z_own]

    def send_partial(i, c):
        z = z_peer(i)
        push(pstage.at[z], pbuf.at[z_own], 6, seq=x_own * N_Z + z)
        return c

    lax.fori_loop(1, N_Z, send_partial, 0)
    drain(recv_sems, 6, pbuf.at[pl.ds(0, N_Z - 1)])
    whole = pbuf[0].astype(F32)
    for i in range(1, N_Z):
        whole = whole + pbuf[i].astype(F32)
    stats = whole[2 * LOCAL_SLOTS :]
    stats = stats + pltpu.roll(stats, 64, 1)
    inv_rms = lax.rsqrt((stats[:, 40:41] + stats[:, 41:42]) / D + 1e-6)
    powers = jnp.where(mask_z[...] > 0.5, jnp.exp(stats * inv_rms), 0.0)
    gates = powers / jnp.sum(powers, axis=1, keepdims=True)
    gates = jnp.where(iota((TOKENS, 128), 1) == 64, inv_rms, gates)
    gates = jnp.concatenate([gates, jnp.zeros((128 - TOKENS, 128), F32)], axis=0)
    gates_high = gates.astype(BF16)
    gates_low = (gates - gates_high.astype(F32)).astype(BF16)
    per_slot = nn_dot(gather_z[...], gates_high) + nn_dot(gather_z[...], gates_low)
    row, col = iota((LOCAL_SLOTS, 128), 0), iota((LOCAL_SLOTS, 128), 1)
    own_gate = jnp.where(col == ex * EXPERTS_LOCAL + row // OWN_SLOTS, per_slot, 0.0)
    gate_weight = jnp.sum(own_gate, axis=1, keepdims=True)
    slot_rms = per_slot[:, 64:65]
    gate = whole[0:LOCAL_SLOTS] * slot_rms
    up = whole[LOCAL_SLOTS : 2 * LOCAL_SLOTS] * slot_rms
    istage[...] = (gate / (1.0 + jnp.exp(-gate)) * up * gate_weight).astype(BF16)
    ibuf[z_own] = istage[...]

    def send_inner(i, c):
        push(istage, ibuf.at[z_own], 7, seq=x_own * N_Z + z_peer(i))
        return c

    lax.fori_loop(1, N_Z, send_inner, 0)
    drain(recv_sems, 7, ibuf.at[pl.ds(0, N_Z - 1)])
    inner = []
    for j in range(EXPERTS_LOCAL):
        at = OWN_SLOTS * j
        slots = ibuf[:, at : at + OWN_SLOTS, :].reshape(SLOTS, 128)
        inner.append(nn_dot(spread_t[j], slots).astype(BF16))
    outputs = nt_dot(down[...], jnp.concatenate(inner, axis=1))
    for x in range(N_X):
        for e in range(N_EXP):
            cols = slice(128 * (e // 4), 128 * (e // 4) + 128)
            at = SLICE * x
            groups = [outputs[at + 16 * b : at + 16 * b + 16, cols] for b in range(3)]
            zstage[x, e] = pack(groups, e % 4).astype(BF16)
    zbuf[x_own, ex] = zstage[x_own, ex]

    def send_z(i, c):
        x, e = plane_peer(i)
        push(zstage.at[x, e], zbuf.at[x_own, ex], 9, seq=x * N_Z + z_own, exp=e)
        return c

    lax.fori_loop(1, N_PLANE, send_z, 0)
    drain_plane(recv_sems, 9)
    moe = jnp.sum(zbuf[...].reshape(N_PLANE, 16, 128).astype(F32), axis=0)
    for b in range(3):
        flip[16 * b : 16 * b + 16, :] = turn(moe, -b)
    flip[0:SLICE, 0:TOKENS] = flip[0:SLICE, 0:TOKENS] + hid[...]
    out = flip[...].T
    out_ref[...] = out[0:TOKENS, 0:SLICE].reshape(STEPS, REQS, SLICE).astype(BF16)

    drain(send_sems, 0, recv1.at[pl.ds(0, N_SEQ - 1)])
    drain(send_sems, 1, mbuf.at[pl.ds(0, N_EXP - 1)])
    drain(send_sems, 3, recv2.at[pl.ds(0, N_SEQ - 1)])
    drain_plane(send_sems, 4)
    drain(send_sems, 2, wbuf.at[pl.ds(0, N_X - 1)])
    drain(send_sems, 10, rbuf.at[pl.ds(0, N_X - 1)])
    drain(send_sems, 6, pbuf.at[pl.ds(0, N_Z - 1)])
    drain(send_sems, 7, ibuf.at[pl.ds(0, N_Z - 1)])
    drain_plane(send_sems, 9)


def layer(page_table, cache_len, *arrays):
    smem = pl.BlockSpec(memory_space=pltpu.SMEM)
    hbm = pl.BlockSpec(memory_space=pltpu.HBM)
    return pl.pallas_call(
        layer_kernel,
        out_shape=jax.ShapeDtypeStruct((STEPS, REQS, SLICE), BF16),
        in_specs=[smem, smem] + [hbm] * 10,
        out_specs=pl.BlockSpec(memory_space=pltpu.VMEM),
        scratch_shapes=[
            VMEM((STEPS, REQS, D), BF16),
            VMEM((STEPS, REQS, 2, 512), BF16),
            VMEM((4, 64, 64, 2, 128), BF16),
            VMEM((SLICE, D), BF16),
            VMEM((STEPS, REQS, SLICE), BF16),
            VMEM((1, SLICE), F32),
            VMEM((EXPERTS, SLICE), BF16),
            VMEM((EXPERTS_LOCAL, SLICE, 2, 512), BF16),
            VMEM((EXPERTS_LOCAL, SLICE, 512), BF16),
            VMEM((STEPS, REQS, 8), jnp.int32),
            VMEM((TOKENS, D), F32),
            VMEM((2, 16, 512), F32),
            VMEM((N_SEQ, 16, 128), F32),
            VMEM((128, 128), F32),
            VMEM((N_SEQ, 16, 128), F32),
            VMEM((16, 128), BF16),
            VMEM((N_SEQ, 16, 128), BF16),
            VMEM((N_SEQ * 16, 128), F32),
            VMEM((N_X, EXPERTS_LOCAL, SLICE, 384), BF16),
            VMEM((N_X, EXPERTS_LOCAL, SLICE, 384), BF16),
            VMEM((N_X, SLICE, 128), BF16),
            VMEM((SLICE, 128), BF16),
            VMEM((N_EXP, SLICE, 128), BF16),
            VMEM((16, 128), BF16),
            VMEM((N_X, N_EXP, 16, 128), BF16),
            VMEM((SLICE, ALL_TOKENS), F32),
            VMEM((SLICE, 128), F32),
            VMEM((EXPERTS_LOCAL, SLOTS, ALL_TOKENS), BF16),
            VMEM((EXPERTS_LOCAL, ALL_TOKENS, SLOTS), BF16),
            VMEM((LOCAL_SLOTS, 128), BF16),
            VMEM((TOKENS, 128), F32),
            VMEM((PLANE, 128 * EXPERTS_LOCAL), BF16),
            VMEM((N_X, SLICE, ALL_TOKENS), BF16),
            VMEM((N_Z, 2 * LOCAL_SLOTS + TOKENS, 128), BF16),
            VMEM((N_Z, 2 * LOCAL_SLOTS + TOKENS, 128), BF16),
            VMEM((LOCAL_SLOTS, 128), BF16),
            VMEM((N_Z, LOCAL_SLOTS, 128), BF16),
            VMEM((N_X, N_EXP, 16, 128), BF16),
            VMEM((N_X, N_EXP, 16, 128), BF16),
            VMEM((SLICE, TOKENS), F32),
            pltpu.SemaphoreType.DMA((9,)),
            pltpu.SemaphoreType.DMA((32,)),
            pltpu.SemaphoreType.DMA((11,)),
            pltpu.SemaphoreType.DMA((11,)),
        ],
        compiler_params=pltpu.CompilerParams(
            collective_id=0, has_side_effects=True, vmem_limit_bytes=60 << 20
        ),
        name="layer",
    )(page_table, cache_len, *arrays)


def local(
    queries,
    new_key_value,
    key_value_cache,
    page_table,
    cache_len,
    routes,
    residual,
    w_out,
    norm_gain,
    w_router,
    w_gate_up,
    w_down,
):
    cache = key_value_cache.reshape(64, 64, 2, 4, 128).transpose(0, 1, 3, 2, 4)
    return layer(
        page_table, cache_len, queries, new_key_value, cache, w_out.T, residual, norm_gain.reshape(1, SLICE),
        w_router.T, w_gate_up, w_down, routes,
    )


def solution(mesh):
    in_specs = (
        P(None, "exp", None),
        P(None, "exp", None, None),
        P("exp", "seq", None, None, None),
        P("exp", "seq"),
        P("exp"),
        P(None, "exp", None),
        P(None, "exp", "seq"),
        P(None, "seq"),
        P("seq"),
        P("seq", None),
        P("exp", "seq", None, None),
        P("exp", "seq", None),
    )
    out_specs = P(None, "exp", "seq")
    return jax.shard_map(local, mesh=mesh, in_specs=in_specs, out_specs=out_specs, check_vma=False)
```

```python
import jax
import jax.numpy as jnp
from jax import lax
from jax.experimental import pallas as pl
from jax.experimental.pallas import tpu as pltpu
from jax.sharding import PartitionSpec as P

NEG = -1e30
N_SEQ = 32
N_EXP = 8
STEPS = 4
REQS = 8
TOKENS = STEPS * REQS
EXPERTS = 40
EXPERTS_LOCAL = 5
OWN_SLOTS = 16
LOCAL_SLOTS = EXPERTS_LOCAL * OWN_SLOTS
TOGETHER = 2
SLOTS = 128
SLICE = 48
N_X = 4
N_Z = 8
PLANE = N_X * SLICE
N_PLANE = N_X * N_EXP
D = 1536
ALL_TOKENS = TOKENS * N_EXP
F32 = jnp.float32
BF16 = jnp.bfloat16
MESH = pl.DeviceIdType.MESH
VMEM = pltpu.VMEM


def iota(shape, axis):
    return lax.broadcasted_iota(jnp.int32, shape, axis)


def nt_dot(a, b):
    return lax.dot_general(a, b, (((1,), (1,)), ((), ())), preferred_element_type=F32)


def nn_dot(a, b):
    return lax.dot_general(a, b, (((1,), (0,)), ((), ())), preferred_element_type=F32)


def spread_queries(q_ref, rows_ref):
    low = iota((REQS, 128), 1) < 64
    for t in range(STEPS):
        q = q_ref[t].astype(F32) * 0.125
        tiles = [q[:, 128 * i : 128 * i + 128] for i in range(12)]
        for g in range(3):
            for pair in range(4):
                first, second = 6 * pair + g, 6 * pair + 3 + g
                if g == 1:
                    tile = jnp.where(low, tiles[second // 2], tiles[first // 2])
                    tile = pltpu.roll(tile, 64, 1)
                else:
                    tile = jnp.where(low, tiles[first // 2], tiles[second // 2])
                base = g * 512 + pair * 128
                rows_ref[REQS * t : REQS * t + REQS, base : base + 128] = tile


def block_diagonal(rows_ref, row, g):
    own = iota((8, 512), 1) // 64 == iota((8, 512), 0)
    values = rows_ref[pl.ds(row, 1), 512 * g : 512 * g + 512]
    return jnp.where(own, jnp.broadcast_to(values, (8, 512)), 0.0)


def softmax_parts(queries, keys, values, live):
    scores = jnp.where(live, nt_dot(queries, keys), NEG)
    largest = jnp.max(scores, axis=1, keepdims=True)
    weights = jnp.exp(scores - jnp.where(largest > 0.5 * NEG, largest, 0.0))
    total = jnp.sum(weights, axis=1, keepdims=True)
    if values is None:
        acc = nn_dot(pltpu.roll(weights, 1, 1).astype(BF16), keys)
    else:
        acc = nn_dot(weights.astype(BF16), values)
    some = total > 0.0
    safe = jnp.where(some, total, 1.0)
    return acc / safe, jnp.where(some, largest + jnp.log(safe), NEG)


def message_tiles(out, lse, groups):
    out = out.reshape(groups, 8, 512)
    lse = lse.reshape(groups, 8, 1)
    head = iota((groups, 8, 128), 1)
    lane = iota((groups, 8, 128), 2)
    packed = out[:, :, 0:128]
    for j in range(1, 4):
        packed = jnp.where(head // 2 == j, out[:, :, 128 * j : 128 * j + 128], packed)
    packed = jnp.where(lane // 64 == head % 2, packed, 0.0)
    head, lane = head[0], lane[0]
    free = lane // 64 != head % 2
    place = lane % 64
    tiles = []
    for t in range(groups // 3):
        first = packed[3 * t] + pltpu.roll(packed[3 * t + 1], 64, 1)
        stat = jnp.where(place == 0, lse[3 * t], jnp.where(place == 1, lse[3 * t + 1], lse[3 * t + 2]))
        second = packed[3 * t + 2] + jnp.where(free & (place < 3), stat, 0.0)
        tiles.append((first, second))
    return tiles


def layer_kernel(
    table_ref, len_ref, q_hbm, new_hbm, kv_hbm, wo_hbm, res_hbm, gain_hbm, wr_hbm, wgu_hbm, wd_hbm, routes_hbm,
    out_ref,
    q_ref, new_ref, pages, wo_ref, res_ref, gain_ref, wr_ref, wgu_ref, wd_ref, routes_ref,
    rows, fresh, msg, flip, recv1, send2, recv2, attf, wstage, wbuf, rbuf, mstage, mbuf, xstage, xbuf,
    slot, slot_z, spread, spread_t, gather_z, mask_z, down, xq, pstage, pbuf, istage, ibuf,
    zstage, zbuf, hid, in_sems, page_sems, send_sems, recv_sems,
):
    me = lax.axis_index("seq")
    ex = lax.axis_index("exp")
    x_own, z_own = lax.div(me, N_Z), lax.rem(me, N_Z)

    def seq_peer(i):
        return lax.rem(me + i, N_SEQ)

    def exp_peer(i):
        return lax.rem(ex + i, N_EXP)

    def x_peer(i):
        return lax.rem(x_own + i, N_X)

    def plane_peer(i):
        place = lax.rem(x_own * N_EXP + ex + i, N_PLANE)
        return lax.div(place, N_EXP), lax.rem(place, N_EXP)

    def z_peer(i):
        return lax.rem(z_own + i, N_Z)

    def push(src, dst, phase, seq=None, exp=None):
        target = (me if seq is None else seq, ex if exp is None else exp)
        pltpu.make_async_remote_copy(
            src_ref=src, dst_ref=dst, send_sem=send_sems.at[phase], recv_sem=recv_sems.at[phase],
            device_id=target, device_id_type=MESH,
        ).start()

    def drain(sems, phase, ref):
        pltpu.make_async_copy(ref, ref, sems.at[phase]).wait()

    loads = [
        pltpu.make_async_copy(src, dst, in_sems.at[i])
        for i, (src, dst) in enumerate(
            (
                (wgu_hbm, wgu_ref), (wd_hbm, wd_ref), (res_hbm, res_ref), (gain_hbm, gain_ref), (wr_hbm, wr_ref),
                (routes_hbm, routes_ref), (q_hbm, q_ref), (new_hbm, new_ref), (wo_hbm, wo_ref),
            )
        )
    ]
    for load in loads:
        load.start()
    page_loads = [
        pltpu.make_async_copy(
            kv_hbm.at[8 * i : 8 * i + 8, :, c], pages.at[c, 8 * i : 8 * i + 8], page_sems.at[4 * i + c]
        )
        for i in range(8)
        for c in range(4)
    ]
    for load in page_loads:
        load.start()

    lane16 = iota((16, 128), 1)

    def turn(tile, quarters):
        return pltpu.roll(tile, 32 * (quarters % 4), 1) if quarters % 4 else tile

    def pack(groups, quarter):
        packed = turn(groups[2], 2 - quarter)
        for b in range(2):
            packed = jnp.where(lane16 // 32 == b, turn(groups[b], b - quarter), packed)
        return packed

    def drain_plane(sems, phase):
        drain(sems, phase, recv2.at[pl.ds(0, N_PLANE - 1)])

    barrier = pltpu.get_barrier_semaphore()

    def greet_seq(i, c):
        pl.semaphore_signal(barrier, inc=1, device_id=(seq_peer(i), ex), device_id_type=MESH)
        return c

    def greet_plane(i, c):
        x, e = plane_peer(i)
        pl.semaphore_signal(barrier, inc=1, device_id=(x * N_Z + z_own, e), device_id_type=MESH)
        return c

    lax.fori_loop(1, N_SEQ, greet_seq, 0)
    lax.fori_loop(1, N_PLANE, greet_plane, 0)

    for load in loads[2:6]:
        load.wait()
    flip[...] = jnp.zeros_like(flip)
    flip[0:TOKENS, 0:SLICE] = res_ref[...].reshape(TOKENS, SLICE).astype(F32)
    flip[TOKENS : TOKENS + 1, 0:SLICE] = gain_ref[...]
    flip[40:80, 0:SLICE] = wr_ref[...].astype(F32)
    flip[0:TOKENS, 64:72] = routes_ref[...].reshape(TOKENS, 8).astype(F32)
    turned = flip[...].T
    top = turned[0:SLICE]
    lane48 = iota((SLICE, 128), 1)
    residual = top[:, 0:TOKENS]
    gain = top[:, TOKENS : TOKENS + 1]
    inv_gain = 1.0 / (gain * gain)
    inv_high = inv_gain.astype(BF16).astype(F32)
    router = pltpu.roll(top, 88, 1)
    router = jnp.where(lane48 == 40, inv_high, jnp.where(lane48 == 41, inv_gain - inv_high, router))
    router = jnp.where(lane48 < 42, router, 0.0).astype(BF16)
    expert_row = iota((SLICE, 128), 0).astype(F32)
    chosen = jnp.zeros((SLICE, 128), F32)
    for k in range(8):
        chosen = jnp.where(expert_row == turned[64 + k : 65 + k, :], 1.0, chosen)
    mstage[...] = chosen.astype(BF16)
    mbuf[ex] = chosen.astype(BF16)

    def send_mask(i, c):
        push(mstage, mbuf.at[ex], 1, exp=exp_peer(i))
        return c

    def send_weights(i, c):
        x = x_peer(i)
        push(wstage.at[x], wbuf.at[x_own], 2, seq=x * N_Z + z_own)
        push(rbuf.at[x_own], rbuf.at[x_own], 10, seq=x * N_Z + z_own)
        return c

    for load in loads[6:8]:
        load.wait()
    spread_queries(q_ref, rows)
    t_own, r_own = lax.div(me, 8), lax.rem(me, 8)
    fresh[...] = jnp.zeros_like(fresh)
    for u in range(STEPS):
        for kind in range(2):
            fresh[kind, u : u + 1, :] = new_ref[u, r_own, kind : kind + 1, :].astype(F32)
    queries = jnp.concatenate([block_diagonal(rows, me, g) for g in range(3)], axis=0).astype(BF16)
    live = iota((24, 16), 1) <= t_own
    out, lse = softmax_parts(queries, fresh[0].astype(BF16), fresh[1].astype(BF16), live)
    ((fresh_first, fresh_second),) = message_tiles(out, lse, 3)

    for load in page_loads:
        load.wait()

    def attend(r):
        both = jnp.concatenate(
            [
                jnp.concatenate([pages[c, table_ref[r, j]].reshape(128, 128) for j in range(8)], axis=0)
                for c in range(4)
            ],
            axis=1,
        )
        queries = jnp.concatenate(
            [block_diagonal(rows, REQS * t + r, g) for t in range(STEPS) for g in range(3)], axis=0
        ).astype(BF16)
        lane = iota((96, 1024), 1)
        live = (lane // 2 + me * 512 < len_ref[r]) & (lane % 2 == 0)
        out, lse = softmax_parts(queries, both, None, live)
        for t, (first, second) in enumerate(message_tiles(out, lse, 12)):
            msg[REQS * t + r, 0:8, :] = first
            msg[REQS * t + r, 8:16, :] = second

    def attend_some(step, c):
        requests = [lax.rem(z_own + 4 + step, N_Z), lax.rem(z_own + 11 - step, N_Z)]
        for r in requests:
            attend(r)

        @pl.when(step == 0)
        def _():
            pl.semaphore_wait(barrier, N_SEQ + N_PLANE - 2)
            lax.fori_loop(1, N_EXP, send_mask, 0)

        for r in requests:
            for t in range(STEPS):
                d = REQS * t + r

                @pl.when(d != me)
                def _():
                    push(msg.at[d], recv1.at[me], 0, seq=d)

        return c

    lax.fori_loop(0, REQS // TOGETHER, attend_some, 0)
    for load in loads[:2]:
        load.wait()
    for j in range(EXPERTS_LOCAL):
        for c in range(N_X):
            cols = slice(128 * c, 128 * c + 128)
            wstage[c, j, :, 0:128] = wgu_ref[j, :, 0, cols]
            wstage[c, j, :, 128:256] = wgu_ref[j, :, 1, cols]
            wstage[c, j, :, 256:384] = wd_ref[j, :, cols]
    wbuf[x_own] = wstage[x_own]
    rbuf[x_own] = router
    lax.fori_loop(1, N_X, send_weights, 0)
    recv1[me] = msg[me]

    loads[8].wait()
    low = iota((SLICE, 128), 1) < 64

    def wo_tile(i):
        return wo_ref[:, 128 * i : 128 * i + 128].astype(F32)

    tiles = []
    for k in range(8):
        if k % 2 == 0:
            tiles.append(wo_tile(3 * k // 2))
        else:
            tiles.append(jnp.where(low, wo_tile((3 * k + 1) // 2), wo_tile((3 * k - 1) // 2)))
    for k in range(8):
        tiles.append(wo_tile((3 * k + 2) // 2))
    wo = jnp.concatenate(tiles, axis=1).astype(BF16)

    def join(ref):
        halves = []
        for h in range(2):
            joined = ref[4 * h].astype(F32)
            for i in range(1, 4):
                part = pltpu.roll(ref[4 * h + i].astype(F32), 32 * i, 1)
                joined = jnp.where(lane48 // 32 == i, part, joined)
            halves.append(joined)
        return jnp.concatenate(halves, axis=1)

    drain(recv_sems, 1, mbuf.at[pl.ds(0, N_EXP - 1)])
    mask = join(mbuf)
    row, col = iota((ALL_TOKENS, ALL_TOKENS), 0), iota((ALL_TOKENS, ALL_TOKENS), 1)
    earlier = jnp.where((row // 8 == col // 8) & (row < col), 1.0, 0.0).astype(BF16)
    rank = nn_dot(mask.astype(BF16), earlier)
    group = (iota((SLICE, ALL_TOKENS), 1) // 8 * 4).astype(F32)
    slot[...] = jnp.where(mask > 0.5, group + rank, -1.0)
    slot_row = iota((SLOTS, ALL_TOKENS), 0).astype(F32)
    for j in range(EXPERTS_LOCAL):
        slots = slot[pl.ds(ex * EXPERTS_LOCAL + j, 1), :]
        hot = jnp.where(slot_row == slots, 1.0, 0.0).astype(BF16)
        spread[j] = hot
        spread_t[j] = hot.T
    mask_one = mbuf[z_own]
    row, col = iota((128, 128), 0), iota((128, 128), 1)
    earlier = jnp.where((row // 8 == col // 8) & (row < col), 1.0, 0.0).astype(BF16)
    rank = nn_dot(mask_one, earlier)
    group = (lane48 // 8 * 4).astype(F32)
    slot_z[...] = jnp.where((mask_one.astype(F32) > 0.5) & (lane48 < TOKENS), group + rank, -1.0)
    slot_row = iota((OWN_SLOTS, 128), 0).astype(F32)
    for j in range(EXPERTS_LOCAL):
        slots = slot_z[pl.ds(ex * EXPERTS_LOCAL + j, 1), :]
        gather_z[OWN_SLOTS * j : OWN_SLOTS * j + OWN_SLOTS, :] = jnp.where(slot_row == slots, 1.0, 0.0).astype(BF16)
    flip[...] = jnp.zeros_like(flip)
    flip[0:SLICE, :] = mask_one.astype(F32)
    mask_z[...] = flip[...].T[0:TOKENS]

    drain(recv_sems, 0, recv1.at[pl.ds(0, N_SEQ - 1)])
    head = iota((8, 128), 0)
    lane = iota((8, 128), 1)
    odd = head % 2 == 1
    half = lane // 64 == head % 2

    def stat_of(second):
        return jnp.where(odd, second, pltpu.roll(second, 64, 1))

    largest = lax.fori_loop(
        0, N_SEQ, lambda s, m: jnp.maximum(m, stat_of(recv1[s, 8:16, :])), stat_of(fresh_second), unroll=8
    )

    def add_part(first, second, carry):
        total, acc1, acc2 = carry
        w = jnp.exp(stat_of(second) - largest)
        w1 = jnp.where(half, w[:, 0:1], w[:, 1:2])
        return total + w, acc1 + w1 * first, acc2 + w[:, 2:3] * second

    zero = jnp.zeros((8, 128), F32)
    carry = add_part(fresh_first, fresh_second, (zero, zero, zero))
    total, acc1, acc2 = lax.fori_loop(
        0, N_SEQ, lambda s, c: add_part(recv1[s, 0:8, :], recv1[s, 8:16, :], c), carry, unroll=8
    )
    att1 = acc1 / jnp.where(half, total[:, 0:1], total[:, 1:2])
    att2 = jnp.where(half, acc2 / total[:, 2:3], 0.0)
    token = jnp.concatenate([att1, att2], axis=0).astype(BF16)
    send2[...] = token
    recv2[me] = token

    def send_token(i, c):
        push(send2, recv2.at[me], 3, seq=seq_peer(lax.rem(i + 10, N_SEQ - 1) + 1))
        return c

    lax.fori_loop(1, N_SEQ, send_token, 0)

    drain(recv_sems, 3, recv2.at[pl.ds(0, N_SEQ - 1)])
    attf[...] = recv2[...].astype(F32).reshape(N_SEQ * 16, 128)
    att = jnp.concatenate([attf[pl.ds(j, N_SEQ, stride=16), :] for j in range(16)], axis=1).astype(BF16)
    hidden = residual + nt_dot(wo, att)
    hid[...] = hidden
    flip[0:SLICE, 0:TOKENS] = hidden * gain
    scaled = flip[0:SLICE, :]
    xstage[...] = pack([scaled[16 * b : 16 * b + 16] for b in range(3)], 0).astype(BF16)
    xbuf[x_own, ex] = xstage[...]

    def send_x(i, c):
        x, e = plane_peer(lax.rem(i + 10, N_PLANE - 1) + 1)
        push(xstage, xbuf.at[x_own, ex], 4, seq=x * N_Z + z_own, exp=e)
        return c

    lax.fori_loop(1, N_PLANE, send_x, 0)

    drain(recv_sems, 2, wbuf.at[pl.ds(0, N_X - 1)])
    drain(recv_sems, 10, rbuf.at[pl.ds(0, N_X - 1)])
    for j in range(EXPERTS_LOCAL):
        down[:, 128 * j : 128 * j + 128] = wbuf[:, j, :, 256:384].reshape(PLANE, 128)
    drain_plane(recv_sems, 4)
    for x in range(N_X):
        for h in range(2):
            blocks = [xbuf[x, 4 * h + i].astype(F32) for i in range(4)]
            for b in range(3):
                joined = turn(blocks[0], -b)
                for i in range(1, 4):
                    joined = jnp.where(lane16 // 32 == i, turn(blocks[i], i - b), joined)
                xq[x, 16 * b : 16 * b + 16, 128 * h : 128 * h + 128] = joined.astype(BF16)
    x_plane = xq[...].reshape(PLANE, ALL_TOKENS)
    for j in range(EXPERTS_LOCAL):
        x_slots = nt_dot(spread[j], x_plane).astype(BF16)
        pre = nn_dot(x_slots, wbuf[:, j, :, 0:256].reshape(PLANE, 256)).astype(BF16)
        at = OWN_SLOTS * j
        pstage[:, at : at + OWN_SLOTS, :] = pre[:, 0:128].reshape(N_Z, OWN_SLOTS, 128)
        at += LOCAL_SLOTS
        pstage[:, at : at + OWN_SLOTS, :] = pre[:, 128:256].reshape(N_Z, OWN_SLOTS, 128)
    same = iota((ALL_TOKENS, ALL_TOKENS), 0) == iota((ALL_TOKENS, ALL_TOKENS), 1)
    x_tokens = nt_dot(jnp.where(same, 1.0, 0.0).astype(BF16), x_plane)
    routing = rbuf[...].reshape(PLANE, 128)
    stats = jnp.where(
        iota((ALL_TOKENS, 128), 1) < EXPERTS,
        nn_dot(x_tokens.astype(BF16), routing),
        nn_dot((x_tokens * x_tokens).astype(BF16), routing),
    )
    stats = jnp.where(iota((ALL_TOKENS, 128), 1) < 42, stats, 0.0)
    stats_high = stats.astype(BF16).astype(F32)
    stats = stats_high + pltpu.roll(stats - stats_high, 64, 1)
    pstage[:, 2 * LOCAL_SLOTS :, :] = stats.astype(BF16).reshape(N_Z, TOKENS, 128)
    pbuf[z_own] = pstage[z_own]

    def send_partial(i, c):
        z = z_peer(i)
        push(pstage.at[z], pbuf.at[z_own], 6, seq=x_own * N_Z + z)
        return c

    for i in (4, 3, 5, 2, 6, 1, 7):
        send_partial(i, 0)
    drain(recv_sems, 6, pbuf.at[pl.ds(0, N_Z - 1)])
    whole = pbuf[0].astype(F32)
    for i in range(1, N_Z):
        whole = whole + pbuf[i].astype(F32)
    stats = whole[2 * LOCAL_SLOTS :]
    stats = stats + pltpu.roll(stats, 64, 1)
    inv_rms = lax.rsqrt((stats[:, 40:41] + stats[:, 41:42]) / D + 1e-6)
    powers = jnp.where(mask_z[...] > 0.5, jnp.exp(stats * inv_rms), 0.0)
    gates = powers / jnp.sum(powers, axis=1, keepdims=True)
    gates = jnp.where(iota((TOKENS, 128), 1) == 64, inv_rms, gates)
    gates = jnp.concatenate([gates, jnp.zeros((128 - TOKENS, 128), F32)], axis=0)
    gates_high = gates.astype(BF16)
    gates_low = (gates - gates_high.astype(F32)).astype(BF16)
    per_slot = nn_dot(gather_z[...], gates_high) + nn_dot(gather_z[...], gates_low)
    row, col = iota((LOCAL_SLOTS, 128), 0), iota((LOCAL_SLOTS, 128), 1)
    own_gate = jnp.where(col == ex * EXPERTS_LOCAL + row // OWN_SLOTS, per_slot, 0.0)
    gate_weight = jnp.sum(own_gate, axis=1, keepdims=True)
    slot_rms = per_slot[:, 64:65]
    gate = whole[0:LOCAL_SLOTS] * slot_rms
    up = whole[LOCAL_SLOTS : 2 * LOCAL_SLOTS] * slot_rms
    istage[...] = (gate / (1.0 + jnp.exp(-gate)) * up * gate_weight).astype(BF16)
    ibuf[z_own] = istage[...]

    def send_inner(i, c):
        push(istage, ibuf.at[z_own], 7, seq=x_own * N_Z + z_peer(i))
        return c

    for i in (4, 3, 5, 2, 6, 1, 7):
        send_inner(i, 0)
    drain(recv_sems, 7, ibuf.at[pl.ds(0, N_Z - 1)])
    inner = []
    for j in range(EXPERTS_LOCAL):
        at = OWN_SLOTS * j
        slots = ibuf[:, at : at + OWN_SLOTS, :].reshape(SLOTS, 128)
        inner.append(nn_dot(spread_t[j], slots).astype(BF16))
    outputs = nt_dot(down[...], jnp.concatenate(inner, axis=1))
    for x in range(N_X):
        for e in range(N_EXP):
            cols = slice(128 * (e // 4), 128 * (e // 4) + 128)
            at = SLICE * x
            groups = [outputs[at + 16 * b : at + 16 * b + 16, cols] for b in range(3)]
            zstage[x, e] = pack(groups, e % 4).astype(BF16)
    zbuf[x_own, ex] = zstage[x_own, ex]

    def send_z(i, c):
        x, e = plane_peer(lax.rem(i + 10, N_PLANE - 1) + 1)
        push(zstage.at[x, e], zbuf.at[x_own, ex], 9, seq=x * N_Z + z_own, exp=e)
        return c

    lax.fori_loop(1, N_PLANE, send_z, 0)
    drain_plane(recv_sems, 9)
    moe = jnp.sum(zbuf[...].reshape(N_PLANE, 16, 128).astype(F32), axis=0)
    for b in range(3):
        flip[16 * b : 16 * b + 16, :] = turn(moe, -b)
    flip[0:SLICE, 0:TOKENS] = flip[0:SLICE, 0:TOKENS] + hid[...]
    out = flip[...].T
    out_ref[...] = out[0:TOKENS, 0:SLICE].reshape(STEPS, REQS, SLICE).astype(BF16)

    drain(send_sems, 0, recv1.at[pl.ds(0, N_SEQ - 1)])
    drain(send_sems, 1, mbuf.at[pl.ds(0, N_EXP - 1)])
    drain(send_sems, 3, recv2.at[pl.ds(0, N_SEQ - 1)])
    drain_plane(send_sems, 4)
    drain(send_sems, 2, wbuf.at[pl.ds(0, N_X - 1)])
    drain(send_sems, 10, rbuf.at[pl.ds(0, N_X - 1)])
    drain(send_sems, 6, pbuf.at[pl.ds(0, N_Z - 1)])
    drain(send_sems, 7, ibuf.at[pl.ds(0, N_Z - 1)])
    drain_plane(send_sems, 9)


def layer(page_table, cache_len, *arrays):
    smem = pl.BlockSpec(memory_space=pltpu.SMEM)
    hbm = pl.BlockSpec(memory_space=pltpu.HBM)
    return pl.pallas_call(
        layer_kernel,
        out_shape=jax.ShapeDtypeStruct((STEPS, REQS, SLICE), BF16),
        in_specs=[smem, smem] + [hbm] * 10,
        out_specs=pl.BlockSpec(memory_space=pltpu.VMEM),
        scratch_shapes=[
            VMEM((STEPS, REQS, D), BF16),
            VMEM((STEPS, REQS, 2, 512), BF16),
            VMEM((4, 64, 64, 2, 128), BF16),
            VMEM((SLICE, D), BF16),
            VMEM((STEPS, REQS, SLICE), BF16),
            VMEM((1, SLICE), F32),
            VMEM((EXPERTS, SLICE), BF16),
            VMEM((EXPERTS_LOCAL, SLICE, 2, 512), BF16),
            VMEM((EXPERTS_LOCAL, SLICE, 512), BF16),
            VMEM((STEPS, REQS, 8), jnp.int32),
            VMEM((TOKENS, D), F32),
            VMEM((2, 16, 512), F32),
            VMEM((N_SEQ, 16, 128), F32),
            VMEM((128, 128), F32),
            VMEM((N_SEQ, 16, 128), F32),
            VMEM((16, 128), BF16),
            VMEM((N_SEQ, 16, 128), BF16),
            VMEM((N_SEQ * 16, 128), F32),
            VMEM((N_X, EXPERTS_LOCAL, SLICE, 384), BF16),
            VMEM((N_X, EXPERTS_LOCAL, SLICE, 384), BF16),
            VMEM((N_X, SLICE, 128), BF16),
            VMEM((SLICE, 128), BF16),
            VMEM((N_EXP, SLICE, 128), BF16),
            VMEM((16, 128), BF16),
            VMEM((N_X, N_EXP, 16, 128), BF16),
            VMEM((SLICE, ALL_TOKENS), F32),
            VMEM((SLICE, 128), F32),
            VMEM((EXPERTS_LOCAL, SLOTS, ALL_TOKENS), BF16),
            VMEM((EXPERTS_LOCAL, ALL_TOKENS, SLOTS), BF16),
            VMEM((LOCAL_SLOTS, 128), BF16),
            VMEM((TOKENS, 128), F32),
            VMEM((PLANE, 128 * EXPERTS_LOCAL), BF16),
            VMEM((N_X, SLICE, ALL_TOKENS), BF16),
            VMEM((N_Z, 2 * LOCAL_SLOTS + TOKENS, 128), BF16),
            VMEM((N_Z, 2 * LOCAL_SLOTS + TOKENS, 128), BF16),
            VMEM((LOCAL_SLOTS, 128), BF16),
            VMEM((N_Z, LOCAL_SLOTS, 128), BF16),
            VMEM((N_X, N_EXP, 16, 128), BF16),
            VMEM((N_X, N_EXP, 16, 128), BF16),
            VMEM((SLICE, TOKENS), F32),
            pltpu.SemaphoreType.DMA((9,)),
            pltpu.SemaphoreType.DMA((32,)),
            pltpu.SemaphoreType.DMA((11,)),
            pltpu.SemaphoreType.DMA((11,)),
        ],
        compiler_params=pltpu.CompilerParams(
            collective_id=0, has_side_effects=True, vmem_limit_bytes=60 << 20
        ),
        name="layer",
    )(page_table, cache_len, *arrays)


def local(
    queries,
    new_key_value,
    key_value_cache,
    page_table,
    cache_len,
    routes,
    residual,
    w_out,
    norm_gain,
    w_router,
    w_gate_up,
    w_down,
):
    cache = key_value_cache.reshape(64, 64, 2, 4, 128).transpose(0, 1, 3, 2, 4)
    return layer(
        page_table, cache_len, queries, new_key_value, cache, w_out.T, residual, norm_gain.reshape(1, SLICE),
        w_router.T, w_gate_up, w_down, routes,
    )


def solution(mesh):
    in_specs = (
        P(None, "exp", None),
        P(None, "exp", None, None),
        P("exp", "seq", None, None, None),
        P("exp", "seq"),
        P("exp"),
        P(None, "exp", None),
        P(None, "exp", "seq"),
        P(None, "seq"),
        P("seq"),
        P("seq", None),
        P("exp", "seq", None, None),
        P("exp", "seq", None),
    )
    out_specs = P(None, "exp", "seq")
    return jax.shard_map(local, mesh=mesh, in_specs=in_specs, out_specs=out_specs, check_vma=False)
```

```python
import jax
import jax.numpy as jnp
from jax import lax
from jax.experimental import pallas as pl
from jax.experimental.pallas import tpu as pltpu
from jax.sharding import PartitionSpec as P

NEG = -1e30
N_SEQ = 32
N_EXP = 8
STEPS = 4
REQS = 8
TOKENS = STEPS * REQS
EXPERTS = 40
EXPERTS_LOCAL = 5
OWN_SLOTS = 16
LOCAL_SLOTS = EXPERTS_LOCAL * OWN_SLOTS
TOGETHER = 2
SLOTS = 128
SLICE = 48
N_X = 4
N_Z = 8
PLANE = N_X * SLICE
N_PLANE = N_X * N_EXP
D = 1536
ALL_TOKENS = TOKENS * N_EXP
F32 = jnp.float32
BF16 = jnp.bfloat16
MESH = pl.DeviceIdType.MESH
VMEM = pltpu.VMEM


def iota(shape, axis):
    return lax.broadcasted_iota(jnp.int32, shape, axis)


def nt_dot(a, b):
    return lax.dot_general(a, b, (((1,), (1,)), ((), ())), preferred_element_type=F32)


def nn_dot(a, b):
    return lax.dot_general(a, b, (((1,), (0,)), ((), ())), preferred_element_type=F32)


def spread_queries(q_ref, rows_ref):
    low = iota((REQS, 128), 1) < 64
    for t in range(STEPS):
        q = q_ref[t].astype(F32) * 0.125
        tiles = [q[:, 128 * i : 128 * i + 128] for i in range(12)]
        for g in range(3):
            for pair in range(4):
                first, second = 6 * pair + g, 6 * pair + 3 + g
                if g == 1:
                    tile = jnp.where(low, tiles[second // 2], tiles[first // 2])
                    tile = pltpu.roll(tile, 64, 1)
                else:
                    tile = jnp.where(low, tiles[first // 2], tiles[second // 2])
                base = g * 512 + pair * 128
                rows_ref[REQS * t : REQS * t + REQS, base : base + 128] = tile


def block_diagonal(rows_ref, row, g):
    own = iota((8, 512), 1) // 64 == iota((8, 512), 0)
    values = rows_ref[pl.ds(row, 1), 512 * g : 512 * g + 512]
    return jnp.where(own, jnp.broadcast_to(values, (8, 512)), 0.0)


def softmax_parts(queries, keys, values, live):
    scores = jnp.where(live, nt_dot(queries, keys), NEG)
    largest = jnp.max(scores, axis=1, keepdims=True)
    weights = jnp.exp(scores - jnp.where(largest > 0.5 * NEG, largest, 0.0))
    total = jnp.sum(weights, axis=1, keepdims=True)
    if values is None:
        acc = nn_dot(pltpu.roll(weights, 1, 1).astype(BF16), keys)
    else:
        acc = nn_dot(weights.astype(BF16), values)
    some = total > 0.0
    safe = jnp.where(some, total, 1.0)
    return acc / safe, jnp.where(some, largest + jnp.log(safe), NEG)


def message_tiles(out, lse, groups):
    out = out.reshape(groups, 8, 512)
    lse = lse.reshape(groups, 8, 1)
    head = iota((groups, 8, 128), 1)
    lane = iota((groups, 8, 128), 2)
    packed = out[:, :, 0:128]
    for j in range(1, 4):
        packed = jnp.where(head // 2 == j, out[:, :, 128 * j : 128 * j + 128], packed)
    packed = jnp.where(lane // 64 == head % 2, packed, 0.0)
    head, lane = head[0], lane[0]
    free = lane // 64 != head % 2
    place = lane % 64
    tiles = []
    for t in range(groups // 3):
        first = packed[3 * t] + pltpu.roll(packed[3 * t + 1], 64, 1)
        stat = jnp.where(place == 0, lse[3 * t], jnp.where(place == 1, lse[3 * t + 1], lse[3 * t + 2]))
        second = packed[3 * t + 2] + jnp.where(free & (place < 3), stat, 0.0)
        tiles.append((first, second))
    return tiles


def layer_kernel(
    table_ref, len_ref, q_hbm, new_hbm, kv_hbm, wo_hbm, res_hbm, gain_hbm, wr_hbm, wgu_hbm, wd_hbm, routes_hbm,
    out_ref,
    q_ref, new_ref, pages, wo_ref, res_ref, gain_ref, wr_ref, wgu_ref, wd_ref, routes_ref,
    rows, fresh, msg, flip, recv1, send2, recv2, attf, wstage, wbuf, rbuf, mstage, mbuf, xstage, xbuf,
    slot, slot_z, spread, spread_t, gather_z, mask_z, down, xq, pstage, pbuf, istage, ibuf,
    zstage, zbuf, hid, in_sems, page_sems, send_sems, recv_sems,
):
    me = lax.axis_index("seq")
    ex = lax.axis_index("exp")
    x_own, z_own = lax.div(me, N_Z), lax.rem(me, N_Z)

    def seq_peer(i):
        return lax.rem(me + i, N_SEQ)

    def exp_peer(i):
        return lax.rem(ex + i, N_EXP)

    def x_peer(i):
        return lax.rem(x_own + i, N_X)

    def plane_peer(i):
        place = lax.rem(x_own * N_EXP + ex + i, N_PLANE)
        return lax.div(place, N_EXP), lax.rem(place, N_EXP)

    def z_peer(i):
        return lax.rem(z_own + i, N_Z)

    def push(src, dst, phase, seq=None, exp=None):
        target = (me if seq is None else seq, ex if exp is None else exp)
        pltpu.make_async_remote_copy(
            src_ref=src, dst_ref=dst, send_sem=send_sems.at[phase], recv_sem=recv_sems.at[phase],
            device_id=target, device_id_type=MESH,
        ).start()

    def drain(sems, phase, ref):
        pltpu.make_async_copy(ref, ref, sems.at[phase]).wait()

    loads = [
        pltpu.make_async_copy(src, dst, in_sems.at[i])
        for i, (src, dst) in enumerate(
            (
                (wgu_hbm, wgu_ref), (wd_hbm, wd_ref), (res_hbm, res_ref), (gain_hbm, gain_ref), (wr_hbm, wr_ref),
                (routes_hbm, routes_ref), (q_hbm, q_ref), (new_hbm, new_ref), (wo_hbm, wo_ref),
            )
        )
    ]
    for load in loads:
        load.start()
    page_loads = [
        pltpu.make_async_copy(
            kv_hbm.at[8 * i : 8 * i + 8, :, c], pages.at[c, 8 * i : 8 * i + 8], page_sems.at[4 * i + c]
        )
        for i in range(8)
        for c in range(4)
    ]
    for load in page_loads:
        load.start()

    lane16 = iota((16, 128), 1)

    def turn(tile, quarters):
        return pltpu.roll(tile, 32 * (quarters % 4), 1) if quarters % 4 else tile

    def pack(groups, quarter):
        packed = turn(groups[2], 2 - quarter)
        for b in range(2):
            packed = jnp.where(lane16 // 32 == b, turn(groups[b], b - quarter), packed)
        return packed

    def drain_plane(sems, phase):
        drain(sems, phase, recv2.at[pl.ds(0, N_PLANE - 1)])

    barrier = pltpu.get_barrier_semaphore()

    def greet_seq(i, c):
        pl.semaphore_signal(barrier, inc=1, device_id=(seq_peer(i), ex), device_id_type=MESH)
        return c

    def greet_plane(i, c):
        x, e = plane_peer(i)
        pl.semaphore_signal(barrier, inc=1, device_id=(x * N_Z + z_own, e), device_id_type=MESH)
        return c

    lax.fori_loop(1, N_SEQ, greet_seq, 0)
    lax.fori_loop(1, N_PLANE, greet_plane, 0)

    for load in loads[2:6]:
        load.wait()
    flip[...] = jnp.zeros_like(flip)
    flip[0:TOKENS, 0:SLICE] = res_ref[...].reshape(TOKENS, SLICE).astype(F32)
    flip[TOKENS : TOKENS + 1, 0:SLICE] = gain_ref[...]
    flip[40:80, 0:SLICE] = wr_ref[...].astype(F32)
    flip[0:TOKENS, 64:72] = routes_ref[...].reshape(TOKENS, 8).astype(F32)
    turned = flip[...].T
    top = turned[0:SLICE]
    lane48 = iota((SLICE, 128), 1)
    residual = top[:, 0:TOKENS]
    gain = top[:, TOKENS : TOKENS + 1]
    inv_gain = 1.0 / (gain * gain)
    inv_high = inv_gain.astype(BF16).astype(F32)
    router = pltpu.roll(top, 88, 1)
    router = jnp.where(lane48 == 40, inv_high, jnp.where(lane48 == 41, inv_gain - inv_high, router))
    router = jnp.where(lane48 < 42, router, 0.0).astype(BF16)
    expert_row = iota((SLICE, 128), 0).astype(F32)
    chosen = jnp.zeros((SLICE, 128), F32)
    for k in range(8):
        chosen = jnp.where(expert_row == turned[64 + k : 65 + k, :], 1.0, chosen)
    mstage[...] = chosen.astype(BF16)
    mbuf[ex] = chosen.astype(BF16)

    def send_mask(i, c):
        push(mstage, mbuf.at[ex], 1, exp=exp_peer(i))
        return c

    def send_weights(i, c):
        x = x_peer(i)
        push(wstage.at[x], wbuf.at[x_own], 2, seq=x * N_Z + z_own)
        push(rbuf.at[x_own], rbuf.at[x_own], 10, seq=x * N_Z + z_own)
        return c

    for load in loads[6:8]:
        load.wait()
    spread_queries(q_ref, rows)
    t_own, r_own = lax.div(me, 8), lax.rem(me, 8)
    fresh[...] = jnp.zeros_like(fresh)
    for u in range(STEPS):
        for kind in range(2):
            fresh[kind, u : u + 1, :] = new_ref[u, r_own, kind : kind + 1, :].astype(F32)
    queries = jnp.concatenate([block_diagonal(rows, me, g) for g in range(3)], axis=0).astype(BF16)
    live = iota((24, 16), 1) <= t_own
    out, lse = softmax_parts(queries, fresh[0].astype(BF16), fresh[1].astype(BF16), live)
    ((fresh_first, fresh_second),) = message_tiles(out, lse, 3)

    for load in page_loads:
        load.wait()

    def attend(r):
        both = jnp.concatenate(
            [
                jnp.concatenate([pages[c, table_ref[r, j]].reshape(128, 128) for j in range(8)], axis=0)
                for c in range(4)
            ],
            axis=1,
        )
        queries = jnp.concatenate(
            [block_diagonal(rows, REQS * t + r, g) for t in range(STEPS) for g in range(3)], axis=0
        ).astype(BF16)
        lane = iota((96, 1024), 1)
        live = (lane // 2 + me * 512 < len_ref[r]) & (lane % 2 == 0)
        out, lse = softmax_parts(queries, both, None, live)
        for t, (first, second) in enumerate(message_tiles(out, lse, 12)):
            msg[REQS * t + r, 0:8, :] = first
            msg[REQS * t + r, 8:16, :] = second

    def attend_some(step, c):
        requests = [lax.rem(z_own + 4 + step, N_Z), lax.rem(z_own + 11 - step, N_Z)]
        for r in requests:
            attend(r)

        @pl.when(step == 0)
        def _():
            pl.semaphore_wait(barrier, N_SEQ + N_PLANE - 2)
            lax.fori_loop(1, N_EXP, send_mask, 0)

        for r in requests:
            for t in range(STEPS):
                d = REQS * t + r

                @pl.when(d != me)
                def _():
                    push(msg.at[d], recv1.at[me], 0, seq=d)

        return c

    lax.fori_loop(0, REQS // TOGETHER, attend_some, 0)
    for load in loads[:2]:
        load.wait()
    for j in range(EXPERTS_LOCAL):
        for c in range(N_X):
            cols = slice(128 * c, 128 * c + 128)
            wstage[c, j, :, 0:128] = wgu_ref[j, :, 0, cols]
            wstage[c, j, :, 128:256] = wgu_ref[j, :, 1, cols]
            wstage[c, j, :, 256:384] = wd_ref[j, :, cols]
    wbuf[x_own] = wstage[x_own]
    rbuf[x_own] = router
    lax.fori_loop(1, N_X, send_weights, 0)
    recv1[me] = msg[me]

    loads[8].wait()
    low = iota((SLICE, 128), 1) < 64

    def wo_tile(i):
        return wo_ref[:, 128 * i : 128 * i + 128].astype(F32)

    tiles = []
    for k in range(8):
        if k % 2 == 0:
            tiles.append(wo_tile(3 * k // 2))
        else:
            tiles.append(jnp.where(low, wo_tile((3 * k + 1) // 2), wo_tile((3 * k - 1) // 2)))
    for k in range(8):
        tiles.append(wo_tile((3 * k + 2) // 2))
    wo = jnp.concatenate(tiles, axis=1).astype(BF16)

    def join(ref):
        halves = []
        for h in range(2):
            joined = ref[4 * h].astype(F32)
            for i in range(1, 4):
                part = pltpu.roll(ref[4 * h + i].astype(F32), 32 * i, 1)
                joined = jnp.where(lane48 // 32 == i, part, joined)
            halves.append(joined)
        return jnp.concatenate(halves, axis=1)

    drain(recv_sems, 1, mbuf.at[pl.ds(0, N_EXP - 1)])
    mask = join(mbuf)
    row, col = iota((ALL_TOKENS, ALL_TOKENS), 0), iota((ALL_TOKENS, ALL_TOKENS), 1)
    earlier = jnp.where((row // 8 == col // 8) & (row < col), 1.0, 0.0).astype(BF16)
    rank = nn_dot(mask.astype(BF16), earlier)
    group = (iota((SLICE, ALL_TOKENS), 1) // 8 * 4).astype(F32)
    slot[...] = jnp.where(mask > 0.5, group + rank, -1.0)
    slot_row = iota((SLOTS, ALL_TOKENS), 0).astype(F32)
    for j in range(EXPERTS_LOCAL):
        slots = slot[pl.ds(ex * EXPERTS_LOCAL + j, 1), :]
        hot = jnp.where(slot_row == slots, 1.0, 0.0).astype(BF16)
        spread[j] = hot
        spread_t[j] = hot.T
    mask_one = mbuf[z_own]
    row, col = iota((128, 128), 0), iota((128, 128), 1)
    earlier = jnp.where((row // 8 == col // 8) & (row < col), 1.0, 0.0).astype(BF16)
    rank = nn_dot(mask_one, earlier)
    group = (lane48 // 8 * 4).astype(F32)
    slot_z[...] = jnp.where((mask_one.astype(F32) > 0.5) & (lane48 < TOKENS), group + rank, -1.0)
    slot_row = iota((OWN_SLOTS, 128), 0).astype(F32)
    for j in range(EXPERTS_LOCAL):
        slots = slot_z[pl.ds(ex * EXPERTS_LOCAL + j, 1), :]
        gather_z[OWN_SLOTS * j : OWN_SLOTS * j + OWN_SLOTS, :] = jnp.where(slot_row == slots, 1.0, 0.0).astype(BF16)
    flip[...] = jnp.zeros_like(flip)
    flip[0:SLICE, :] = mask_one.astype(F32)
    mask_z[...] = flip[...].T[0:TOKENS]

    drain(recv_sems, 0, recv1.at[pl.ds(0, N_SEQ - 1)])
    head = iota((8, 128), 0)
    lane = iota((8, 128), 1)
    odd = head % 2 == 1
    half = lane // 64 == head % 2

    def stat_of(second):
        return jnp.where(odd, second, pltpu.roll(second, 64, 1))

    largest = lax.fori_loop(
        0, N_SEQ, lambda s, m: jnp.maximum(m, stat_of(recv1[s, 8:16, :])), stat_of(fresh_second), unroll=8
    )

    def add_part(first, second, carry):
        total, acc1, acc2 = carry
        w = jnp.exp(stat_of(second) - largest)
        w1 = jnp.where(half, w[:, 0:1], w[:, 1:2])
        return total + w, acc1 + w1 * first, acc2 + w[:, 2:3] * second

    zero = jnp.zeros((8, 128), F32)
    carry = add_part(fresh_first, fresh_second, (zero, zero, zero))
    total, acc1, acc2 = lax.fori_loop(
        0, N_SEQ, lambda s, c: add_part(recv1[s, 0:8, :], recv1[s, 8:16, :], c), carry, unroll=8
    )
    att1 = acc1 / jnp.where(half, total[:, 0:1], total[:, 1:2])
    att2 = jnp.where(half, acc2 / total[:, 2:3], 0.0)
    token = jnp.concatenate([att1, att2], axis=0).astype(BF16)
    send2[...] = token
    recv2[me] = token

    def send_token(i, c):
        push(send2, recv2.at[me], 3, seq=seq_peer(lax.rem(i + 10, N_SEQ - 1) + 1))
        return c

    lax.fori_loop(1, N_SEQ, send_token, 0)

    drain(recv_sems, 3, recv2.at[pl.ds(0, N_SEQ - 1)])
    attf[...] = recv2[...].astype(F32).reshape(N_SEQ * 16, 128)
    att = jnp.concatenate([attf[pl.ds(j, N_SEQ, stride=16), :] for j in range(16)], axis=1).astype(BF16)
    hidden = residual + nt_dot(wo, att)
    hid[...] = hidden
    flip[0:SLICE, 0:TOKENS] = hidden * gain
    scaled = flip[0:SLICE, :]
    xstage[...] = pack([scaled[16 * b : 16 * b + 16] for b in range(3)], 0).astype(BF16)
    xbuf[x_own, ex] = xstage[...]

    def send_x(i, c):
        x, e = plane_peer(lax.rem(i + 10, N_PLANE - 1) + 1)
        push(xstage, xbuf.at[x_own, ex], 4, seq=x * N_Z + z_own, exp=e)
        return c

    lax.fori_loop(1, N_PLANE, send_x, 0)

    drain(recv_sems, 2, wbuf.at[pl.ds(0, N_X - 1)])
    drain(recv_sems, 10, rbuf.at[pl.ds(0, N_X - 1)])
    for j in range(EXPERTS_LOCAL):
        down[:, 128 * j : 128 * j + 128] = wbuf[:, j, :, 256:384].reshape(PLANE, 128)
    drain_plane(recv_sems, 4)
    for x in range(N_X):
        for h in range(2):
            blocks = [xbuf[x, 4 * h + i].astype(F32) for i in range(4)]
            for b in range(3):
                joined = turn(blocks[0], -b)
                for i in range(1, 4):
                    joined = jnp.where(lane16 // 32 == i, turn(blocks[i], i - b), joined)
                xq[x, 16 * b : 16 * b + 16, 128 * h : 128 * h + 128] = joined.astype(BF16)
    x_plane = xq[...].reshape(PLANE, ALL_TOKENS)

    def send_rows(at, count):
        for i in (4, 3, 5, 2, 6, 1, 7):
            z = z_peer(i)
            here, there = pstage.at[z, pl.ds(at, count)], pbuf.at[z_own, pl.ds(at, count)]
            push(here, there, 6, seq=x_own * N_Z + z)

    for j in range(EXPERTS_LOCAL):
        x_slots = nt_dot(spread[j], x_plane).astype(BF16)
        pre = nn_dot(x_slots, wbuf[:, j, :, 0:256].reshape(PLANE, 256)).astype(BF16)
        at = 2 * OWN_SLOTS * j
        pstage[:, at : at + OWN_SLOTS, :] = pre[:, 0:128].reshape(N_Z, OWN_SLOTS, 128)
        pstage[:, at + OWN_SLOTS : at + 2 * OWN_SLOTS, :] = pre[:, 128:256].reshape(N_Z, OWN_SLOTS, 128)
        send_rows(at, 2 * OWN_SLOTS)
    same = iota((ALL_TOKENS, ALL_TOKENS), 0) == iota((ALL_TOKENS, ALL_TOKENS), 1)
    x_tokens = nt_dot(jnp.where(same, 1.0, 0.0).astype(BF16), x_plane)
    routing = rbuf[...].reshape(PLANE, 128)
    stats = jnp.where(
        iota((ALL_TOKENS, 128), 1) < EXPERTS,
        nn_dot(x_tokens.astype(BF16), routing),
        nn_dot((x_tokens * x_tokens).astype(BF16), routing),
    )
    stats = jnp.where(iota((ALL_TOKENS, 128), 1) < 42, stats, 0.0)
    stats_high = stats.astype(BF16).astype(F32)
    stats = stats_high + pltpu.roll(stats - stats_high, 64, 1)
    pstage[:, 2 * LOCAL_SLOTS :, :] = stats.astype(BF16).reshape(N_Z, TOKENS, 128)
    pbuf[z_own] = pstage[z_own]

    send_rows(2 * LOCAL_SLOTS, TOKENS)
    drain(recv_sems, 6, pbuf.at[pl.ds(0, N_Z - 1)])
    whole = pbuf[0].astype(F32)
    for i in range(1, N_Z):
        whole = whole + pbuf[i].astype(F32)
    stats = whole[2 * LOCAL_SLOTS :]
    stats = stats + pltpu.roll(stats, 64, 1)
    inv_rms = lax.rsqrt((stats[:, 40:41] + stats[:, 41:42]) / D + 1e-6)
    powers = jnp.where(mask_z[...] > 0.5, jnp.exp(stats * inv_rms), 0.0)
    gates = powers / jnp.sum(powers, axis=1, keepdims=True)
    gates = jnp.where(iota((TOKENS, 128), 1) == 64, inv_rms, gates)
    gates = jnp.concatenate([gates, jnp.zeros((128 - TOKENS, 128), F32)], axis=0)
    gates_high = gates.astype(BF16)
    gates_low = (gates - gates_high.astype(F32)).astype(BF16)
    per_slot = nn_dot(gather_z[...], gates_high) + nn_dot(gather_z[...], gates_low)
    row, col = iota((LOCAL_SLOTS, 128), 0), iota((LOCAL_SLOTS, 128), 1)
    own_gate = jnp.where(col == ex * EXPERTS_LOCAL + row // OWN_SLOTS, per_slot, 0.0)
    gate_weight = jnp.sum(own_gate, axis=1, keepdims=True)
    slot_rms = per_slot[:, 64:65]
    sums = whole[0 : 2 * LOCAL_SLOTS].reshape(EXPERTS_LOCAL, 2, OWN_SLOTS, 128)
    gate = sums[:, 0].reshape(LOCAL_SLOTS, 128) * slot_rms
    up = sums[:, 1].reshape(LOCAL_SLOTS, 128) * slot_rms
    istage[...] = (gate / (1.0 + jnp.exp(-gate)) * up * gate_weight).astype(BF16)
    ibuf[z_own] = istage[...]

    def send_inner(i, c):
        push(istage, ibuf.at[z_own], 7, seq=x_own * N_Z + z_peer(i))
        return c

    for i in (4, 3, 5, 2, 6, 1, 7):
        send_inner(i, 0)
    drain(recv_sems, 7, ibuf.at[pl.ds(0, N_Z - 1)])
    inner = []
    for j in range(EXPERTS_LOCAL):
        at = OWN_SLOTS * j
        slots = ibuf[:, at : at + OWN_SLOTS, :].reshape(SLOTS, 128)
        inner.append(nn_dot(spread_t[j], slots).astype(BF16))
    outputs = nt_dot(down[...], jnp.concatenate(inner, axis=1))
    for x in range(N_X):
        for e in range(N_EXP):
            cols = slice(128 * (e // 4), 128 * (e // 4) + 128)
            at = SLICE * x
            groups = [outputs[at + 16 * b : at + 16 * b + 16, cols] for b in range(3)]
            zstage[x, e] = pack(groups, e % 4).astype(BF16)
    zbuf[x_own, ex] = zstage[x_own, ex]

    def send_z(i, c):
        x, e = plane_peer(lax.rem(i + 10, N_PLANE - 1) + 1)
        push(zstage.at[x, e], zbuf.at[x_own, ex], 9, seq=x * N_Z + z_own, exp=e)
        return c

    lax.fori_loop(1, N_PLANE, send_z, 0)
    drain_plane(recv_sems, 9)
    moe = jnp.sum(zbuf[...].reshape(N_PLANE, 16, 128).astype(F32), axis=0)
    for b in range(3):
        flip[16 * b : 16 * b + 16, :] = turn(moe, -b)
    flip[0:SLICE, 0:TOKENS] = flip[0:SLICE, 0:TOKENS] + hid[...]
    out = flip[...].T
    out_ref[...] = out[0:TOKENS, 0:SLICE].reshape(STEPS, REQS, SLICE).astype(BF16)

    drain(send_sems, 0, recv1.at[pl.ds(0, N_SEQ - 1)])
    drain(send_sems, 1, mbuf.at[pl.ds(0, N_EXP - 1)])
    drain(send_sems, 3, recv2.at[pl.ds(0, N_SEQ - 1)])
    drain_plane(send_sems, 4)
    drain(send_sems, 2, wbuf.at[pl.ds(0, N_X - 1)])
    drain(send_sems, 10, rbuf.at[pl.ds(0, N_X - 1)])
    drain(send_sems, 6, pbuf.at[pl.ds(0, N_Z - 1)])
    drain(send_sems, 7, ibuf.at[pl.ds(0, N_Z - 1)])
    drain_plane(send_sems, 9)


def layer(page_table, cache_len, *arrays):
    smem = pl.BlockSpec(memory_space=pltpu.SMEM)
    hbm = pl.BlockSpec(memory_space=pltpu.HBM)
    return pl.pallas_call(
        layer_kernel,
        out_shape=jax.ShapeDtypeStruct((STEPS, REQS, SLICE), BF16),
        in_specs=[smem, smem] + [hbm] * 10,
        out_specs=pl.BlockSpec(memory_space=pltpu.VMEM),
        scratch_shapes=[
            VMEM((STEPS, REQS, D), BF16),
            VMEM((STEPS, REQS, 2, 512), BF16),
            VMEM((4, 64, 64, 2, 128), BF16),
            VMEM((SLICE, D), BF16),
            VMEM((STEPS, REQS, SLICE), BF16),
            VMEM((1, SLICE), F32),
            VMEM((EXPERTS, SLICE), BF16),
            VMEM((EXPERTS_LOCAL, SLICE, 2, 512), BF16),
            VMEM((EXPERTS_LOCAL, SLICE, 512), BF16),
            VMEM((STEPS, REQS, 8), jnp.int32),
            VMEM((TOKENS, D), F32),
            VMEM((2, 16, 512), F32),
            VMEM((N_SEQ, 16, 128), F32),
            VMEM((128, 128), F32),
            VMEM((N_SEQ, 16, 128), F32),
            VMEM((16, 128), BF16),
            VMEM((N_SEQ, 16, 128), BF16),
            VMEM((N_SEQ * 16, 128), F32),
            VMEM((N_X, EXPERTS_LOCAL, SLICE, 384), BF16),
            VMEM((N_X, EXPERTS_LOCAL, SLICE, 384), BF16),
            VMEM((N_X, SLICE, 128), BF16),
            VMEM((SLICE, 128), BF16),
            VMEM((N_EXP, SLICE, 128), BF16),
            VMEM((16, 128), BF16),
            VMEM((N_X, N_EXP, 16, 128), BF16),
            VMEM((SLICE, ALL_TOKENS), F32),
            VMEM((SLICE, 128), F32),
            VMEM((EXPERTS_LOCAL, SLOTS, ALL_TOKENS), BF16),
            VMEM((EXPERTS_LOCAL, ALL_TOKENS, SLOTS), BF16),
            VMEM((LOCAL_SLOTS, 128), BF16),
            VMEM((TOKENS, 128), F32),
            VMEM((PLANE, 128 * EXPERTS_LOCAL), BF16),
            VMEM((N_X, SLICE, ALL_TOKENS), BF16),
            VMEM((N_Z, 2 * LOCAL_SLOTS + TOKENS, 128), BF16),
            VMEM((N_Z, 2 * LOCAL_SLOTS + TOKENS, 128), BF16),
            VMEM((LOCAL_SLOTS, 128), BF16),
            VMEM((N_Z, LOCAL_SLOTS, 128), BF16),
            VMEM((N_X, N_EXP, 16, 128), BF16),
            VMEM((N_X, N_EXP, 16, 128), BF16),
            VMEM((SLICE, TOKENS), F32),
            pltpu.SemaphoreType.DMA((9,)),
            pltpu.SemaphoreType.DMA((32,)),
            pltpu.SemaphoreType.DMA((11,)),
            pltpu.SemaphoreType.DMA((11,)),
        ],
        compiler_params=pltpu.CompilerParams(
            collective_id=0, has_side_effects=True, vmem_limit_bytes=60 << 20
        ),
        name="layer",
    )(page_table, cache_len, *arrays)


def local(
    queries,
    new_key_value,
    key_value_cache,
    page_table,
    cache_len,
    routes,
    residual,
    w_out,
    norm_gain,
    w_router,
    w_gate_up,
    w_down,
):
    cache = key_value_cache.reshape(64, 64, 2, 4, 128).transpose(0, 1, 3, 2, 4)
    return layer(
        page_table, cache_len, queries, new_key_value, cache, w_out.T, residual, norm_gain.reshape(1, SLICE),
        w_router.T, w_gate_up, w_down, routes,
    )


def solution(mesh):
    in_specs = (
        P(None, "exp", None),
        P(None, "exp", None, None),
        P("exp", "seq", None, None, None),
        P("exp", "seq"),
        P("exp"),
        P(None, "exp", None),
        P(None, "exp", "seq"),
        P(None, "seq"),
        P("seq"),
        P("seq", None),
        P("exp", "seq", None, None),
        P("exp", "seq", None),
    )
    out_specs = P(None, "exp", "seq")
    return jax.shard_map(local, mesh=mesh, in_specs=in_specs, out_specs=out_specs, check_vma=False)
```
